128 devices in a mesh: pts: 8 (over y, z_lo), lmk: 16 (over z_hi, x, core).
Axes of the slice: x: 4, y: 4, z: 4 (z_hi: 2, z_lo: 2; z = z_hi * 2 + z_lo), core: 2. Of those that a mesh axis runs over, the one named last changes fastest.
Arguments:
- points: float32 [32768, 384], P('pts'), may hold values from -8 to 8
- labels: int32 [32768], P('pts'), may hold values from 0 to 127
- landmarks: float32 [32768, 384], P('lmk'), may hold values from -8 to 8
- coefficients: float32 [32768, 128], P('lmk'), may hold values from -3 to 3
Outputs:
- gradient: float32 [32768, 128], P('lmk')
The draws below stay inside these ranges and needn't reach their ends.
All inputs are finite; a program needn't handle non-finite values.
Results may differ from the reference program's by a relative error of at most 0.0003.
Values sent between devices are 32-bit elements; how exact they have to be, the bound alone decides.
No kernel may reach another device: no remote copies, remote signals or barrier semaphores. Data moves between devices by JAX's collectives and lax.ppermute only.
A program may use at most 128 MiB of HBM per device.

```python
import jax
import jax.numpy as jnp
from jax import lax

F = 384
K = 128
NP_DEV = 4096
NPTS = 32768
M = 32768
N_PTS = 8


cluster_count = 64


latent_rank = 4


latent_spread = 0.7071


noise_level = 0.5


value_limit = 8.0


def cluster_layout(key):
    maps = jax.random.truncated_normal(jax.random.fold_in(key, 8), -3.0, 3.0, (cluster_count, latent_rank, F), jnp.float32) * latent_spread
    centres = jax.random.truncated_normal(jax.random.fold_in(key, 7), -3.0, 3.0, (cluster_count, F), jnp.float32)
    return (centres, maps)


def point_members(key):
    return jax.random.randint(jax.random.fold_in(key, 11), (NPTS,), 0, cluster_count)


def landmark_members(key):
    return jax.random.randint(jax.random.fold_in(key, 13), (M,), 0, cluster_count)


def place_members(key, member, salt):
    high = lax.Precision.HIGHEST
    centres, maps = cluster_layout(key)
    count = member.shape[0]
    latent = jax.random.truncated_normal(jax.random.fold_in(key, salt), -3.0, 3.0, (count, latent_rank), jnp.float32)
    noise = jax.random.truncated_normal(jax.random.fold_in(key, salt + 1), -3.0, 3.0, (count, F), jnp.float32) * noise_level
    selector = (member[:, None] == jnp.arange(cluster_count, dtype=jnp.int32)[None, :]).astype(jnp.float32)
    spread_in = (selector[:, :, None] * latent[:, None, :]).reshape(count, cluster_count * latent_rank)
    spread = jnp.dot(spread_in, maps.reshape(cluster_count * latent_rank, F), precision=high)
    base = jnp.dot(selector, centres, precision=high)
    values = base + spread + noise
    return jnp.clip(values, -value_limit, value_limit)


def draw_points(key, part):
    return place_members(key, point_members(key), 21)


def draw_landmarks(key, part):
    return place_members(key, landmark_members(key), 31)


def draw_labels(key, part):
    member = point_members(key)
    class_of = jax.random.randint(jax.random.fold_in(key, 12), (cluster_count,), 0, K)
    mixing = jax.random.randint(jax.random.fold_in(key, 14), (NPTS,), 0, 4)
    others = jax.random.randint(jax.random.fold_in(key, 15), (NPTS,), 0, K)
    return jnp.where(mixing > 0, class_of[member], others).astype(jnp.int32)


def steps_of(key, extent, pieces, low, high):
    gain, own = 1.0, jax.random.fold_in(key, 6)
    for position, shards_of in pieces:
        draws = jnp.exp(jax.random.uniform(jax.random.fold_in(own, position), (shards_of,), jnp.float32, low / len(pieces), high / len(pieces)))
        gain = gain * jnp.repeat(draws, extent[position] // shards_of).reshape([-1 if axis == position else 1 for axis in range(len(extent))])
    return gain


def gaussian(rng, extent, deviation, limit, shards=(), held_as=jnp.bfloat16):
    values = deviation * jax.random.normal(rng, extent, jnp.float32)
    if shards:
        values = values * steps_of(rng, extent, shards, -0.22, 0.18)
    return jnp.clip(values, -limit, limit).astype(held_as)


def setup_inputs(seed: int = 0) -> dict:
    key_of = jax.random.split(jax.random.key(seed), 5)
    points = draw_points(jax.random.fold_in(key_of[4], 71), 0)
    labels = draw_labels(jax.random.fold_in(key_of[4], 71), 0)
    landmarks = draw_landmarks(jax.random.fold_in(key_of[4], 71), 0)
    coefficients = gaussian(key_of[3], (M, K), (max(1, M // 8192)) ** -0.5, 3.0, ((0, 16),), jnp.float32)
    return {"points": points, "labels": labels, "landmarks": landmarks, "coefficients": coefficients}


LOSS_SCALE = 8192.0
RIDGE = 0.5


def reference(points, labels, landmarks, coefficients):
    high = lax.Precision.HIGHEST
    feats = points.shape[1]
    total_points = points.shape[0]
    lnorm = jnp.sum(landmarks * landmarks, axis=1)
    blocks_pts = points.reshape(N_PTS, NP_DEV, feats)
    blocks_lab = labels.reshape(N_PTS, NP_DEV)
    classes = coefficients.shape[1]

    def step(carry, block):
        pblock, lblock = block
        pnorm = jnp.sum(pblock * pblock, axis=1)
        cross = jnp.dot(pblock, landmarks.T, precision=high, preferred_element_type=jnp.float32)
        kernel = jnp.exp(-(pnorm[:, None] + lnorm[None, :] - 2.0 * cross) / feats)
        logits = jnp.dot(kernel, coefficients, precision=high, preferred_element_type=jnp.float32)
        expo = jnp.exp(logits)
        onehot = (lblock[:, None] == jnp.arange(classes, dtype=jnp.int32)[None, :]).astype(jnp.float32)
        resid = expo / jnp.sum(expo, axis=1, keepdims=True) - onehot
        term = lax.dot_general(kernel, resid, (((0,), (0,)), ((), ())), precision=high, preferred_element_type=jnp.float32)
        return carry + term, None

    start = jnp.zeros(coefficients.shape, jnp.float32)
    summed, unused = lax.scan(step, start, (blocks_pts, blocks_lab))
    return summed * (LOSS_SCALE / total_points) + RIDGE * coefficients
```

```python
import functools
import math

import jax
import jax.numpy as jnp
from jax import lax
from jax.experimental import pallas as pl
from jax.experimental.pallas import tpu as pltpu
from jax.sharding import Mesh
from jax.sharding import PartitionSpec as P

LOSS_SCALE = 8192.0
RIDGE = 0.5
LANES = 128
AXES = ("y", "zl", "zh", "x", "core")
PTS = ("y", "zl")
CHIPS = ("zh", "x")
LMK = ("zh", "x", "core")
NT = (((1,), (1,)), ((), ()))
f32, bf16 = jnp.float32, jnp.bfloat16


def dot(a, b):
    return jnp.dot(a, b, preferred_element_type=f32)


def halves(x):
    high = x.astype(bf16)
    return high, (x - high.astype(f32)).astype(bf16)


def thirds(x):
    a = x.astype(bf16).astype(f32)
    b = (x - a).astype(bf16).astype(f32)
    return a, b, x - a - b


def norm_lanes(rows, columns):
    lane = lax.broadcasted_iota(jnp.int32, (rows, LANES), 1)
    out = jnp.zeros((rows, LANES), f32)
    for i, column in enumerate(columns):
        out = jnp.where(lane == i, column, out)
    return out.astype(bf16)


def prep_body(l_ref, c_ref, b_ref, cc_ref):
    rows, feats = l_ref.shape
    unit = math.log2(math.e) / feats
    mark = l_ref[...]
    high, low = halves(mark * (2.0 * unit))
    b_ref[:, :feats] = high
    b_ref[:, feats : 2 * feats] = low
    b_ref[:, 2 * feats : 3 * feats] = high
    norm = thirds(-unit * jnp.sum(mark * mark, axis=1, keepdims=True))
    b_ref[:, 3 * feats :] = norm_lanes(rows, [1.0, 1.0, 1.0, *norm])
    high, low = halves(c_ref[...])
    cc_ref[:, : high.shape[1]] = high
    cc_ref[:, high.shape[1] :] = low


def prep(landmarks, coefficients, block=512):
    marks, feats = landmarks.shape
    classes = coefficients.shape[1]
    wide = 3 * feats + LANES
    return pl.pallas_call(
        prep_body,
        grid=(marks // block,),
        in_specs=[
            pl.BlockSpec((block, feats), lambda i: (i, 0)),
            pl.BlockSpec((block, classes), lambda i: (i, 0)),
        ],
        out_specs=[
            pl.BlockSpec((block, wide), lambda i: (i, 0)),
            pl.BlockSpec((block, 2 * classes), lambda i: (i, 0)),
        ],
        out_shape=[
            jax.ShapeDtypeStruct((marks, wide), bf16),
            jax.ShapeDtypeStruct((marks, 2 * classes), bf16),
        ],
        name="prep",
    )(landmarks, coefficients)


def logits_body(first_ref, p_ref, b_ref, c_ref, hi_ref, lo_ref, out_ref, a_ref, *, tile):
    rows, feats = p_ref.shape
    marks = b_ref.shape[0]
    unit = math.log2(math.e) / feats
    point = p_ref[...]
    high, low = halves(point)
    a_ref[:, :feats] = high
    a_ref[:, feats : 2 * feats] = high
    a_ref[:, 2 * feats : 3 * feats] = low
    norm = thirds(-unit * jnp.sum(point * point, axis=1, keepdims=True))
    a_ref[:, 3 * feats :] = norm_lanes(rows, [*norm, 1.0, 1.0, 1.0])
    for j in range(marks // tile):
        cols = slice(j * tile, (j + 1) * tile)
        power = lax.dot_general(a_ref[...], b_ref[cols, :], NT, preferred_element_type=f32)
        kernel = jnp.exp2(power)
        high, low = halves(kernel)
        hi_ref[:, cols] = high
        lo_ref[:, cols] = low
    for u in range(2):
        part = slice(u * rows // 2, (u + 1) * rows // 2)
        both = dot(hi_ref[part, :], c_ref[...]) + dot(lo_ref[part, :], c_ref[...])
        out_ref[part, :] = both[:, : both.shape[1] // 2] + both[:, both.shape[1] // 2 :]


def kernel_and_logits(first_row, points, wide_marks, wide_coefs, rows, block=512, tile=512):
    feats = points.shape[1]
    marks, wide = wide_marks.shape
    classes = wide_coefs.shape[1] // 2
    fixed = pl.Buffered(1)
    first = (first_row // block).astype(jnp.int32).reshape(1)
    return pl.pallas_call(
        functools.partial(logits_body, tile=tile),
        grid_spec=pltpu.PrefetchScalarGridSpec(
            num_scalar_prefetch=1,
            grid=(rows // block,),
            in_specs=[
                pl.BlockSpec((block, feats), lambda i, s: (s[0] + i, 0)),
                pl.BlockSpec((marks, wide), lambda i, s: (0, 0), pipeline_mode=fixed),
                pl.BlockSpec((marks, 2 * classes), lambda i, s: (0, 0), pipeline_mode=fixed),
            ],
            out_specs=[
                pl.BlockSpec((block, marks), lambda i, s: (i, 0)),
                pl.BlockSpec((block, marks), lambda i, s: (i, 0)),
                pl.BlockSpec((block, classes), lambda i, s: (i, 0)),
            ],
            scratch_shapes=[pltpu.VMEM((block, wide), bf16)],
        ),
        out_shape=[
            jax.ShapeDtypeStruct((rows, marks), bf16),
            jax.ShapeDtypeStruct((rows, marks), bf16),
            jax.ShapeDtypeStruct((rows, classes), f32),
        ],
        cost_estimate=pl.CostEstimate(
            flops=2 * rows * marks * (wide + 4 * classes),
            bytes_accessed=4 * rows * (feats + marks + classes) + 2 * marks * (wide + 2 * classes),
            transcendentals=rows * marks,
        ),
        name="kernel_and_logits",
    )(first, points, wide_marks, wide_coefs)


def terms_body(*refs):
    r_ref, hi_ref, lo_ref, *before, out_ref, rt_ref = refs
    classes = r_ref.shape[1]

    @pl.when(pl.program_id(0) == 0)
    def _():
        resid = r_ref[...]
        high = resid.astype(bf16).astype(f32)
        rt_ref[:classes, :] = high.T.astype(bf16)
        rt_ref[classes:, :] = (resid - high).T.astype(bf16)

    both = dot(rt_ref[...], hi_ref[...]) + dot(rt_ref[...], lo_ref[...])
    out = (both[:classes, :] + both[classes:, :]).T
    for ref in before:
        out = out + ref[...]
    out_ref[...] = out


def terms(resid, high, low, before=None, block=512):
    rows, marks = high.shape
    classes = resid.shape[1]
    ins = [
        pl.BlockSpec((rows, classes), lambda i: (0, 0), pipeline_mode=pl.Buffered(1)),
        pl.BlockSpec((rows, block), lambda i: (0, i)),
        pl.BlockSpec((rows, block), lambda i: (0, i)),
    ]
    args = [resid, high, low]
    out_spec = pl.BlockSpec((block, classes), lambda i: (i, 0))
    if before is not None:
        ins.append(out_spec)
        args.append(before)
    return pl.pallas_call(
        terms_body,
        grid=(marks // block,),
        in_specs=ins,
        out_specs=out_spec,
        out_shape=jax.ShapeDtypeStruct((marks, classes), f32),
        scratch_shapes=[pltpu.VMEM((2 * classes, rows), bf16)],
        cost_estimate=pl.CostEstimate(
            flops=8 * rows * marks * classes,
            bytes_accessed=4 * rows * (marks + classes) + 8 * marks * classes,
            transcendentals=0,
        ),
        name="terms",
    )(*args)


def swapped(x):
    return lax.ppermute(x, "core", [(0, 1), (1, 0)])


def summed_share(x, axes):
    devices = lax.axis_size(axes)
    parts = x.reshape(devices, x.shape[0] // devices, x.shape[1])
    return lax.all_to_all(parts, axes, split_axis=0, concat_axis=0, tiled=True).sum(axis=0)


def all_shares(x, axes):
    devices = lax.axis_size(axes)
    copies = jnp.broadcast_to(x, (devices, *x.shape))
    parts = lax.all_to_all(copies, axes, split_axis=0, concat_axis=0, tiled=True)
    return parts.reshape(devices * x.shape[0], x.shape[1])


def residual_rows(logits, labels):
    classes = logits.shape[1]
    expo = jnp.exp(logits)
    onehot = (labels[:, None] == jnp.arange(classes, dtype=jnp.int32)[None, :]).astype(f32)
    return expo / jnp.sum(expo, axis=1, keepdims=True) - onehot


def per_device(points, labels, landmarks, coefficients):
    rows = points.shape[0] // 2
    core = lax.axis_index("core")
    wide_marks, wide_coefs = prep(landmarks, coefficients)
    far_hi, far_lo, far_logits = kernel_and_logits((1 - core) * rows, points, wide_marks, wide_coefs, rows)
    arrived = swapped(far_logits)
    own_hi, own_lo, own_logits = kernel_and_logits(core * rows, points, wide_marks, wide_coefs, rows)
    shares = summed_share(own_logits + arrived, CHIPS)
    share_rows = shares.shape[0]
    first = core * rows + lax.axis_index(CHIPS) * share_rows
    mine = lax.dynamic_slice_in_dim(labels, first, share_rows, 0)
    own_resid = all_shares(residual_rows(shares, mine), CHIPS)
    far_resid = swapped(own_resid)
    local = terms(own_resid, own_hi, own_lo)
    local = terms(far_resid, far_hi, far_lo, local)
    total_points = labels.shape[0] * lax.axis_size(PTS)
    share = summed_share(local, PTS)
    kept = share.shape[0]
    own_coefs = lax.dynamic_slice_in_dim(coefficients, lax.axis_index(PTS) * kept, kept, 0)
    return all_shares(share * (LOSS_SCALE / total_points) + RIDGE * own_coefs, PTS)


def solution(mesh):
    fine = Mesh(mesh.devices.reshape(4, 2, 2, 4, 2), AXES)
    in_specs = (P(PTS, None), P(PTS), P(LMK, None), P(LMK, None))
    return jax.shard_map(
        per_device, mesh=fine, in_specs=in_specs, out_specs=P(LMK, None), check_vma=False
    )
```

```python
import functools
import math

import jax
import jax.numpy as jnp
from jax import lax
from jax.experimental import pallas as pl
from jax.experimental.pallas import tpu as pltpu
from jax.sharding import Mesh
from jax.sharding import PartitionSpec as P

LOSS_SCALE = 8192.0
RIDGE = 0.5
LIMIT_K1, LIMIT_K2 = 9, 9
LANES = 128
AXES = ("y", "zl", "zh", "x", "core")
PTS = ("y", "zl")
LMK = ("zh", "x", "core")
NT = (((1,), (1,)), ((), ()))
f32, bf16 = jnp.float32, jnp.bfloat16


def dot(a, b):
    return jnp.dot(a, b, preferred_element_type=f32)


def halves(x):
    high = x.astype(bf16)
    return high, (x - high.astype(f32)).astype(bf16)


def thirds(x):
    a = x.astype(bf16).astype(f32)
    b = (x - a).astype(bf16).astype(f32)
    return a, b, x - a - b


def norm_lanes(rows, columns):
    lane = lax.broadcasted_iota(jnp.int32, (rows, LANES), 1)
    out = jnp.zeros((rows, LANES), f32)
    for i, column in enumerate(columns):
        out = jnp.where(lane == i, column, out)
    return out.astype(bf16)


def prep_body(l_ref, c_ref, b_ref, cc_ref):
    rows, feats = l_ref.shape
    unit = math.log2(math.e) / feats
    mark = l_ref[...]
    high, low = halves(mark * (2.0 * unit))
    b_ref[:, :feats] = high
    b_ref[:, feats : 2 * feats] = low
    b_ref[:, 2 * feats : 3 * feats] = high
    norm = thirds(-unit * jnp.sum(mark * mark, axis=1, keepdims=True))
    b_ref[:, 3 * feats :] = norm_lanes(rows, [1.0, 1.0, 1.0, *norm])
    high, low = halves(c_ref[...])
    cc_ref[:, : high.shape[1]] = high
    cc_ref[:, high.shape[1] :] = low


def prep(landmarks, coefficients, block=512):
    marks, feats = landmarks.shape
    classes = coefficients.shape[1]
    wide = 3 * feats + LANES
    return pl.pallas_call(
        prep_body,
        grid=(marks // block,),
        in_specs=[
            pl.BlockSpec((block, feats), lambda i: (i, 0)),
            pl.BlockSpec((block, classes), lambda i: (i, 0)),
        ],
        out_specs=[
            pl.BlockSpec((block, wide), lambda i: (i, 0)),
            pl.BlockSpec((block, 2 * classes), lambda i: (i, 0)),
        ],
        out_shape=[
            pltpu.VMEM((marks, wide), bf16),
            pltpu.VMEM((marks, 2 * classes), bf16),
        ],
        compiler_params=pltpu.CompilerParams(vmem_limit_bytes=12 << 20),
        name="prep",
    )(landmarks, coefficients)


def logits_body(at_ref, p_ref, b_ref, c_ref, hi_ref, lo_ref, far_ref, own_ref, a_ref, *, tile):
    rows, feats = p_ref.shape
    marks = b_ref.shape[0]
    unit = math.log2(math.e) / feats
    point = p_ref[...]
    high, low = halves(point)
    a_ref[:, :feats] = high
    a_ref[:, feats : 2 * feats] = high
    a_ref[:, 2 * feats : 3 * feats] = low
    norm = thirds(-unit * jnp.sum(point * point, axis=1, keepdims=True))
    a_ref[:, 3 * feats :] = norm_lanes(rows, [*norm, 1.0, 1.0, 1.0])
    for j in range(marks // tile):
        cols = slice(j * tile, (j + 1) * tile)
        power = lax.dot_general(a_ref[...], b_ref[cols, :], NT, preferred_element_type=f32)
        kernel = jnp.exp2(power)
        high, low = halves(kernel)
        hi_ref[:, cols] = high
        lo_ref[:, cols] = low
    sums = []
    for u in range(2):
        part = slice(u * rows // 2, (u + 1) * rows // 2)
        both = dot(hi_ref[part, :], c_ref[...]) + dot(lo_ref[part, :], c_ref[...])
        sums.append(both[:, : both.shape[1] // 2] + both[:, both.shape[1] // 2 :])

    @pl.when(pl.program_id(0) == 0)
    def _():
        far_ref[...] = jnp.concatenate(sums, axis=0)

    @pl.when(pl.program_id(0) == 1)
    def _():
        own_ref[...] = jnp.concatenate(sums, axis=0)


def kernel_and_logits(at, shift, points, wide_marks, wide_coefs, block, tile=512):
    feats = points.shape[1]
    marks, wide = wide_marks.shape
    classes = wide_coefs.shape[1] // 2
    chips = points.shape[0] // (2 * block)
    fixed = pl.Buffered(1)
    return pl.pallas_call(
        functools.partial(logits_body, tile=tile),
        grid_spec=pltpu.PrefetchScalarGridSpec(
            num_scalar_prefetch=1,
            grid=(2,),
            in_specs=[
                pl.BlockSpec(
                    (block, feats),
                    lambda i, s: (lax.rem(s[0] + shift, chips) * 2 + lax.rem(s[1] + 1 + i, 2), 0),
                ),
                pl.BlockSpec((marks, wide), lambda i, s: (0, 0), pipeline_mode=fixed),
                pl.BlockSpec((marks, 2 * classes), lambda i, s: (0, 0), pipeline_mode=fixed),
            ],
            out_specs=[
                pl.BlockSpec((block, marks), lambda i, s: (i, 0)),
                pl.BlockSpec((block, marks), lambda i, s: (i, 0)),
                pl.BlockSpec((block, classes), lambda i, s: (0, 0)),
                pl.BlockSpec((block, classes), lambda i, s: (0, 0)),
            ],
            scratch_shapes=[pltpu.VMEM((block, wide), bf16)],
        ),
        out_shape=[
            pltpu.VMEM((2 * block, marks), bf16),
            pltpu.VMEM((2 * block, marks), bf16),
            pltpu.VMEM((block, classes), f32),
            pltpu.VMEM((block, classes), f32),
        ],
        compiler_params=pltpu.CompilerParams(vmem_limit_bytes=LIMIT_K1 << 20),
        cost_estimate=pl.CostEstimate(
            flops=4 * block * marks * (wide + 4 * classes),
            bytes_accessed=8 * block * (feats + marks + classes) + 2 * marks * (wide + 2 * classes),
            transcendentals=2 * block * marks,
        ),
        name="kernel_and_logits",
    )(at, points, wide_marks, wide_coefs)


def small_kernel(body, at, args, outs, name):
    whole = [pl.BlockSpec(x.shape, lambda i, s: (0, 0)) for x in (*args, *outs)]
    return pl.pallas_call(
        body,
        grid_spec=pltpu.PrefetchScalarGridSpec(
            num_scalar_prefetch=1,
            grid=(1,),
            in_specs=whole[: len(args)],
            out_specs=whole[len(args) :],
        ),
        out_shape=outs,
        compiler_params=pltpu.CompilerParams(vmem_limit_bytes=6 << 20),
        name=name,
    )(at, *args)


def split_body(at_ref, *refs):
    *ins, send_ref, keep_ref = refs
    rows = keep_ref.shape[0]
    for ref, which in ((send_ref, 1 - at_ref[2]), (keep_ref, at_ref[2])):
        part = pl.ds(pl.multiple_of(which * rows, rows), rows)
        total = ins[0][part, :]
        for x in ins[1:]:
            total = total + x[part, :]
        ref[...] = total


def residual_body(at_ref, labels_ref, a_ref, b_ref, out_ref):
    logits = a_ref[...] + b_ref[...]
    rows, classes = logits.shape
    groups = rows // LANES
    expo = jnp.exp(logits)
    share = expo / jnp.sum(expo, axis=1, keepdims=True)
    base = (at_ref[0] * 4 + at_ref[1] * 2 + at_ref[2]) * groups
    for g in range(groups):
        label = jnp.broadcast_to(labels_ref[pl.ds(base + g, 1), :], (LANES, LANES)).T
        hot = label == lax.broadcasted_iota(jnp.int32, (LANES, classes), 1)
        part = slice(g * LANES, (g + 1) * LANES)
        out_ref[part, :] = share[part, :] - hot.astype(f32)


def join_body(at_ref, own_ref, other_ref, out_ref):
    rows = own_ref.shape[0]
    for ref, which in ((own_ref, at_ref[2]), (other_ref, 1 - at_ref[2])):
        out_ref[pl.ds(pl.multiple_of(which * rows, rows), rows), :] = ref[...]


def terms_body(*refs, sets, tile):
    parts, (*before, out_ref, rt_ref) = refs[: 4 * sets], refs[4 * sets :]
    classes = parts[0].shape[1]
    block = parts[0].shape[0]
    marks = parts[2].shape[1]
    for n in range(sets):
        for h in range(2):
            resid = parts[4 * n + h][...]
            high = resid.astype(bf16).astype(f32)
            rows = slice((2 * n + h) * block, (2 * n + h + 1) * block)
            rt_ref[:classes, rows] = high.T.astype(bf16)
            rt_ref[classes:, rows] = (resid - high).T.astype(bf16)
    for j in range(marks // tile):
        cols = slice(j * tile, (j + 1) * tile)
        both = None
        for n in range(sets):
            left = rt_ref[:, 2 * n * block : 2 * (n + 1) * block]
            for ref in parts[4 * n + 2 : 4 * n + 4]:
                term = dot(left, ref[:, cols])
                both = term if both is None else both + term
        out = (both[:classes, :] + both[classes:, :]).T
        for ref in before:
            out = out + ref[cols, :]
        out_ref[cols, :] = out


def terms(sets, before=None, tile=512):
    args = [x for one in sets for x in one]
    block, classes = args[0].shape
    marks = args[2].shape[1]
    rows = 2 * block * len(sets)
    if before is not None:
        args.append(before)
    return pl.pallas_call(
        functools.partial(terms_body, sets=len(sets), tile=tile),
        in_specs=[pl.BlockSpec(memory_space=pltpu.VMEM)] * len(args),
        out_specs=pl.BlockSpec(memory_space=pltpu.VMEM),
        out_shape=pltpu.VMEM((marks, classes), f32),
        scratch_shapes=[pltpu.VMEM((2 * classes, rows), bf16)],
        compiler_params=pltpu.CompilerParams(vmem_limit_bytes=LIMIT_K2 << 20),
        cost_estimate=pl.CostEstimate(
            flops=8 * rows * marks * classes,
            bytes_accessed=4 * rows * (marks + classes) + 8 * marks * classes,
            transcendentals=0,
        ),
        name="terms",
    )(*args)


def swapped(x):
    return lax.ppermute(x, "core", [(0, 1), (1, 0)])


def summed_share(x, axes):
    devices = lax.axis_size(axes)
    parts = x.reshape(devices, x.shape[0] // devices, x.shape[1])
    return lax.all_to_all(parts, axes, split_axis=0, concat_axis=0, tiled=True).sum(axis=0)


def all_shares(x, axes):
    devices = lax.axis_size(axes)
    copies = jnp.broadcast_to(x, (devices, *x.shape))
    parts = lax.all_to_all(copies, axes, split_axis=0, concat_axis=0, tiled=True)
    return parts.reshape(devices * x.shape[0], x.shape[1])


def along_x(x, shift):
    chips = lax.axis_size("x")
    return lax.ppermute(x, "x", [(i, (i + shift) % chips) for i in range(chips)])


def across_z(x):
    return lax.ppermute(x, "zh", [(0, 1), (1, 0)])


def per_device(points, labels, landmarks, coefficients):
    chips, layers = lax.axis_size("x"), lax.axis_size("zh")
    classes = coefficients.shape[1]
    block = points.shape[0] // (2 * chips)
    rows = block // layers
    at = jnp.stack([lax.axis_index(n) for n in ("x", "core", "zh")]).astype(jnp.int32)
    points, landmarks, first_coefs = (
        pltpu.with_memory_space_constraint(x, pltpu.HBM) for x in (points, landmarks, coefficients)
    )
    at, landmarks = lax.optimization_barrier((at, landmarks))
    wide_marks, wide_coefs = prep(landmarks, first_coefs)
    made, sums, waiting = {}, [], None
    for shift in (2, 1, 3, 0):
        hi, lo, far, own = kernel_and_logits(at, shift, points, wide_marks, wide_coefs, block)
        made[shift] = hi, lo
        if waiting is not None:
            there, mine, arrived = waiting
            ready = mine + arrived
            at, ready = lax.optimization_barrier((at, ready))
            sums.append(along_x(ready, there))
        waiting = shift, own, swapped(far)
    sums += waiting[1:]
    half = jax.ShapeDtypeStruct((rows, classes), f32)
    send, keep = small_kernel(split_body, at, sums, [half, half], "split")
    by_group = labels.reshape(-1, LANES)
    (resid,) = small_kernel(residual_body, at, [by_group, keep, across_z(send)], [half], "residual")
    full = jax.ShapeDtypeStruct((block, classes), f32)
    (own,) = small_kernel(join_body, at, [resid, across_z(resid)], [full], "join")
    resids = {3: along_x(own, 1), 1: along_x(own, 3), 2: along_x(own, 2)}
    local = terms([(swapped(own), own, *made[0])])
    local, resids = lax.optimization_barrier((local, resids))
    local = terms([(swapped(resids[n]), resids[n], *made[n]) for n in (3, 1, 2)], local)
    total_points = labels.shape[0] * lax.axis_size(PTS)
    share = summed_share(local, PTS)
    kept = share.shape[0]
    own_coefs = lax.dynamic_slice_in_dim(coefficients, lax.axis_index(PTS) * kept, kept, 0)
    return all_shares(share * (LOSS_SCALE / total_points) + RIDGE * own_coefs, PTS)


def solution(mesh):
    fine = Mesh(mesh.devices.reshape(4, 2, 2, 4, 2), AXES)
    in_specs = (P(PTS, None), P(PTS), P(LMK, None), P(LMK, None))
    return jax.shard_map(
        per_device, mesh=fine, in_specs=in_specs, out_specs=P(LMK, None), check_vma=False
    )
```

```python
import functools
import math

import jax
import jax.numpy as jnp
from jax import lax
from jax.experimental import pallas as pl
from jax.experimental.pallas import tpu as pltpu
from jax.sharding import Mesh
from jax.sharding import PartitionSpec as P

LOSS_SCALE = 8192.0
RIDGE = 0.5
LIMIT_K1, LIMIT_K2 = 9, 9
LANES = 128
AXES = ("y", "zl", "zh", "x", "core")
PTS = ("y", "zl")
LMK = ("zh", "x", "core")
NT = (((1,), (1,)), ((), ()))
f32, bf16 = jnp.float32, jnp.bfloat16


def dot(a, b):
    return jnp.dot(a, b, preferred_element_type=f32)


def halves(x):
    high = x.astype(bf16)
    return high, (x - high.astype(f32)).astype(bf16)


def thirds(x):
    a = x.astype(bf16).astype(f32)
    b = (x - a).astype(bf16).astype(f32)
    return a, b, x - a - b


def norm_lanes(rows, columns):
    lane = lax.broadcasted_iota(jnp.int32, (rows, LANES), 1)
    out = jnp.zeros((rows, LANES), f32)
    for i, column in enumerate(columns):
        out = jnp.where(lane == i, column, out)
    return out.astype(bf16)


def prep_body(l_ref, c_ref, b_ref, cc_ref):
    rows, feats = l_ref.shape
    unit = math.log2(math.e) / feats
    mark = l_ref[...]
    high, low = halves(mark * (2.0 * unit))
    b_ref[:, :feats] = high
    b_ref[:, feats : 2 * feats] = low
    b_ref[:, 2 * feats : 3 * feats] = high
    norm = thirds(-unit * jnp.sum(mark * mark, axis=1, keepdims=True))
    b_ref[:, 3 * feats :] = norm_lanes(rows, [1.0, 1.0, 1.0, *norm])
    high, low = halves(c_ref[...])
    cc_ref[:, : high.shape[1]] = high
    cc_ref[:, high.shape[1] :] = low


def prep(landmarks, coefficients, block=512):
    marks, feats = landmarks.shape
    classes = coefficients.shape[1]
    wide = 3 * feats + LANES
    return pl.pallas_call(
        prep_body,
        grid=(marks // block,),
        in_specs=[
            pl.BlockSpec((block, feats), lambda i: (i, 0)),
            pl.BlockSpec((block, classes), lambda i: (i, 0)),
        ],
        out_specs=[
            pl.BlockSpec((block, wide), lambda i: (i, 0)),
            pl.BlockSpec((block, 2 * classes), lambda i: (i, 0)),
        ],
        out_shape=[
            pltpu.VMEM((marks, wide), bf16),
            pltpu.VMEM((marks, 2 * classes), bf16),
        ],
        compiler_params=pltpu.CompilerParams(vmem_limit_bytes=12 << 20),
        name="prep",
    )(landmarks, coefficients)


def logits_body(at_ref, p_ref, b_ref, c_ref, hi_ref, lo_ref, far_ref, own_ref, a_ref, *, tile):
    rows, feats = p_ref.shape
    marks = b_ref.shape[0]
    unit = math.log2(math.e) / feats
    point = p_ref[...]
    high, low = halves(point)
    a_ref[:, :feats] = high
    a_ref[:, feats : 2 * feats] = high
    a_ref[:, 2 * feats : 3 * feats] = low
    norm = thirds(-unit * jnp.sum(point * point, axis=1, keepdims=True))
    a_ref[:, 3 * feats :] = norm_lanes(rows, [*norm, 1.0, 1.0, 1.0])
    for j in range(marks // tile):
        cols = slice(j * tile, (j + 1) * tile)
        power = lax.dot_general(a_ref[...], b_ref[cols, :], NT, preferred_element_type=f32)
        kernel = jnp.exp2(power)
        high, low = halves(kernel)
        hi_ref[:, cols] = high
        lo_ref[:, cols] = low
    sums = []
    for u in range(2):
        part = slice(u * rows // 2, (u + 1) * rows // 2)
        both = dot(hi_ref[part, :], c_ref[...]) + dot(lo_ref[part, :], c_ref[...])
        sums.append(both[:, : both.shape[1] // 2] + both[:, both.shape[1] // 2 :])

    @pl.when(pl.program_id(0) == 0)
    def _():
        far_ref[...] = jnp.concatenate(sums, axis=0)

    @pl.when(pl.program_id(0) == 1)
    def _():
        own_ref[...] = jnp.concatenate(sums, axis=0)


def kernel_and_logits(at, shift, points, wide_marks, wide_coefs, block, tile=512):
    feats = points.shape[1]
    marks, wide = wide_marks.shape
    classes = wide_coefs.shape[1] // 2
    chips = points.shape[0] // (2 * block)
    fixed = pl.Buffered(1)
    return pl.pallas_call(
        functools.partial(logits_body, tile=tile),
        grid_spec=pltpu.PrefetchScalarGridSpec(
            num_scalar_prefetch=1,
            grid=(2,),
            in_specs=[
                pl.BlockSpec(
                    (block, feats),
                    lambda i, s: (lax.rem(s[0] + shift, chips) * 2 + lax.rem(s[1] + 1 + i, 2), 0),
                ),
                pl.BlockSpec((marks, wide), lambda i, s: (0, 0), pipeline_mode=fixed),
                pl.BlockSpec((marks, 2 * classes), lambda i, s: (0, 0), pipeline_mode=fixed),
            ],
            out_specs=[
                pl.BlockSpec((block, marks), lambda i, s: (i, 0)),
                pl.BlockSpec((block, marks), lambda i, s: (i, 0)),
                pl.BlockSpec((block, classes), lambda i, s: (0, 0)),
                pl.BlockSpec((block, classes), lambda i, s: (0, 0)),
            ],
            scratch_shapes=[pltpu.VMEM((block, wide), bf16)],
        ),
        out_shape=[
            pltpu.VMEM((2 * block, marks), bf16),
            pltpu.VMEM((2 * block, marks), bf16),
            pltpu.VMEM((block, classes), f32),
            pltpu.VMEM((block, classes), f32),
        ],
        compiler_params=pltpu.CompilerParams(vmem_limit_bytes=LIMIT_K1 << 20),
        cost_estimate=pl.CostEstimate(
            flops=4 * block * marks * (wide + 4 * classes),
            bytes_accessed=8 * block * (feats + marks + classes) + 2 * marks * (wide + 2 * classes),
            transcendentals=2 * block * marks,
        ),
        name="kernel_and_logits",
    )(at, points, wide_marks, wide_coefs)


def small_kernel(body, at, args, outs, name):
    whole = [pl.BlockSpec(x.shape, lambda i, s: (0, 0)) for x in (*args, *outs)]
    return pl.pallas_call(
        body,
        grid_spec=pltpu.PrefetchScalarGridSpec(
            num_scalar_prefetch=1,
            grid=(1,),
            in_specs=whole[: len(args)],
            out_specs=whole[len(args) :],
        ),
        out_shape=outs,
        compiler_params=pltpu.CompilerParams(vmem_limit_bytes=6 << 20),
        name=name,
    )(at, *args)


def residual_body(at_ref, labels_ref, a_ref, b_ref, out_ref):
    logits = a_ref[...] + b_ref[...]
    rows, classes = logits.shape
    groups = rows // LANES
    expo = jnp.exp(logits)
    share = expo / jnp.sum(expo, axis=1, keepdims=True)
    base = (at_ref[0] * 2 + at_ref[1]) * groups
    for g in range(groups):
        label = jnp.broadcast_to(labels_ref[pl.ds(base + g, 1), :], (LANES, LANES)).T
        hot = label == lax.broadcasted_iota(jnp.int32, (LANES, classes), 1)
        part = slice(g * LANES, (g + 1) * LANES)
        out_ref[part, :] = share[part, :] - hot.astype(f32)


def terms_body(*refs, sets, tile):
    parts, (*before, out_ref, rt_ref) = refs[: 4 * sets], refs[4 * sets :]
    classes = parts[0].shape[1]
    block = parts[0].shape[0]
    marks = parts[2].shape[1]
    for n in range(sets):
        for h in range(2):
            resid = parts[4 * n + h][...]
            high = resid.astype(bf16).astype(f32)
            rows = slice((2 * n + h) * block, (2 * n + h + 1) * block)
            rt_ref[:classes, rows] = high.T.astype(bf16)
            rt_ref[classes:, rows] = (resid - high).T.astype(bf16)
    for j in range(marks // tile):
        cols = slice(j * tile, (j + 1) * tile)
        both = None
        for n in range(sets):
            left = rt_ref[:, 2 * n * block : 2 * (n + 1) * block]
            for ref in parts[4 * n + 2 : 4 * n + 4]:
                term = dot(left, ref[:, cols])
                both = term if both is None else both + term
        out = (both[:classes, :] + both[classes:, :]).T
        for ref in before:
            out = out + ref[cols, :]
        out_ref[cols, :] = out


def terms(sets, before=None, tile=512):
    args = [x for one in sets for x in one]
    block, classes = args[0].shape
    marks = args[2].shape[1]
    rows = 2 * block * len(sets)
    if before is not None:
        args.append(before)
    return pl.pallas_call(
        functools.partial(terms_body, sets=len(sets), tile=tile),
        in_specs=[pl.BlockSpec(memory_space=pltpu.VMEM)] * len(args),
        out_specs=pl.BlockSpec(memory_space=pltpu.VMEM),
        out_shape=pltpu.VMEM((marks, classes), f32),
        scratch_shapes=[pltpu.VMEM((2 * classes, rows), bf16)],
        compiler_params=pltpu.CompilerParams(vmem_limit_bytes=LIMIT_K2 << 20),
        cost_estimate=pl.CostEstimate(
            flops=8 * rows * marks * classes,
            bytes_accessed=4 * rows * (marks + classes) + 8 * marks * classes,
            transcendentals=0,
        ),
        name="terms",
    )(*args)


def swapped(x):
    return lax.ppermute(x, "core", [(0, 1), (1, 0)])


def summed_share(x, axes):
    devices = lax.axis_size(axes)
    parts = x.reshape(devices, x.shape[0] // devices, x.shape[1])
    return lax.all_to_all(parts, axes, split_axis=0, concat_axis=0, tiled=True).sum(axis=0)


def all_shares(x, axes):
    devices = lax.axis_size(axes)
    copies = jnp.broadcast_to(x, (devices, *x.shape))
    parts = lax.all_to_all(copies, axes, split_axis=0, concat_axis=0, tiled=True)
    return parts.reshape(devices * x.shape[0], x.shape[1])


def along_x(x, shift):
    chips = lax.axis_size("x")
    return lax.ppermute(x, "x", [(i, (i + shift) % chips) for i in range(chips)])


def across_z(x):
    return lax.ppermute(x, "zh", [(0, 1), (1, 0)])


def per_device(points, labels, landmarks, coefficients):
    chips = lax.axis_size("x")
    classes = coefficients.shape[1]
    block = points.shape[0] // (2 * chips)
    at = jnp.stack([lax.axis_index(n) for n in ("x", "core")]).astype(jnp.int32)
    points, landmarks, first_coefs = (
        pltpu.with_memory_space_constraint(x, pltpu.HBM) for x in (points, landmarks, coefficients)
    )
    at, landmarks = lax.optimization_barrier((at, landmarks))
    wide_marks, wide_coefs = prep(landmarks, first_coefs)
    made, mine, arrived, sums = {}, {}, {}, []
    for shift, ready in ((2, ()), (1, (2,)), (3, (1, 3)), (0, ())):
        hi, lo, far, own = kernel_and_logits(at, shift, points, wide_marks, wide_coefs, block)
        made[shift] = hi, lo
        mine[shift], arrived[shift] = own, swapped(far)
        both = [mine[n] + arrived[n] for n in ready]
        if both:
            at, both = lax.optimization_barrier((at, both))
        sums += [along_x(x, n) for x, n in zip(both, ready)]
    logits = mine[0] + arrived[0] + sums[0] + sums[1] + sums[2]
    full = jax.ShapeDtypeStruct((block, classes), f32)
    by_group = labels.reshape(-1, LANES)
    (own,) = small_kernel(residual_body, at, [by_group, logits, across_z(logits)], [full], "residual")
    near = {3: along_x(own, 1), 1: along_x(own, 3)}
    local = terms([(swapped(own), own, *made[0])])
    local, near = lax.optimization_barrier((local, near))
    front, back = along_x(near[3][: block // 2], 1), along_x(near[1][block // 2 :], 3)
    local = terms([(swapped(near[n]), near[n], *made[n]) for n in (3, 1)], local)
    local, front, back = lax.optimization_barrier((local, front, back))
    last = jnp.concatenate([front, back], axis=0)
    local = terms([(swapped(last), last, *made[2])], local)
    total_points = labels.shape[0] * lax.axis_size(PTS)
    share = summed_share(local, PTS)
    kept = share.shape[0]
    own_coefs = lax.dynamic_slice_in_dim(coefficients, lax.axis_index(PTS) * kept, kept, 0)
    return all_shares(share * (LOSS_SCALE / total_points) + RIDGE * own_coefs, PTS)


def solution(mesh):
    fine = Mesh(mesh.devices.reshape(4, 2, 2, 4, 2), AXES)
    in_specs = (P(PTS, None), P(PTS), P(LMK, None), P(LMK, None))
    return jax.shard_map(
        per_device, mesh=fine, in_specs=in_specs, out_specs=P(LMK, None), check_vma=False
    )
```

```python
import functools
import math

import jax
import jax.numpy as jnp
from jax import lax
from jax.experimental import pallas as pl
from jax.experimental.pallas import tpu as pltpu
from jax.sharding import Mesh
from jax.sharding import PartitionSpec as P

LOSS_SCALE = 8192.0
RIDGE = 0.5
LIMIT_K1, LIMIT_K2 = 8, 6
LANES = 128
AXES = ("y", "zl", "zh", "x", "core")
PTS = ("y", "zl")
LMK = ("zh", "x", "core")
NT = (((1,), (1,)), ((), ()))
f32, bf16 = jnp.float32, jnp.bfloat16


def dot(a, b):
    return jnp.dot(a, b, preferred_element_type=f32)


def halves(x):
    high = x.astype(bf16)
    return high, (x - high.astype(f32)).astype(bf16)


def thirds(x):
    a = x.astype(bf16).astype(f32)
    b = (x - a).astype(bf16).astype(f32)
    return a, b, x - a - b


def norm_lanes(rows, columns):
    lane = lax.broadcasted_iota(jnp.int32, (rows, LANES), 1)
    out = jnp.zeros((rows, LANES), f32)
    for i, column in enumerate(columns):
        out = jnp.where(lane == i, column, out)
    return out.astype(bf16)


def fetched(at_ref, shift, points_ref, next_ref, sem):
    rows = next_ref.shape[0]
    chips = points_ref.shape[0] // rows
    first = pl.multiple_of(lax.rem(at_ref[0] + shift, chips) * rows, rows)
    return pltpu.make_async_copy(points_ref.at[pl.ds(first, rows), :], next_ref, sem)


def prep_body(at_ref, l_ref, c_ref, points_ref, b_ref, cc_ref, next_ref, sem, *, shift):
    copy = fetched(at_ref, shift, points_ref, next_ref, sem)

    @pl.when(pl.program_id(0) == 0)
    def _():
        copy.start()

    rows, feats = l_ref.shape
    unit = math.log2(math.e) / feats
    mark = l_ref[...]
    high, low = halves(mark * (2.0 * unit))
    b_ref[:, :feats] = high
    b_ref[:, feats : 2 * feats] = low
    b_ref[:, 2 * feats : 3 * feats] = high
    norm = thirds(-unit * jnp.sum(mark * mark, axis=1, keepdims=True))
    b_ref[:, 3 * feats :] = norm_lanes(rows, [1.0, 1.0, 1.0, *norm])
    high, low = halves(c_ref[...])
    cc_ref[:, : high.shape[1]] = high
    cc_ref[:, high.shape[1] :] = low

    @pl.when(pl.program_id(0) == pl.num_programs(0) - 1)
    def _():
        copy.wait()


def prep(at, shift, landmarks, coefficients, points, held_rows, block=512):
    marks, feats = landmarks.shape
    classes = coefficients.shape[1]
    wide = 3 * feats + LANES
    return pl.pallas_call(
        functools.partial(prep_body, shift=shift),
        grid_spec=pltpu.PrefetchScalarGridSpec(
            num_scalar_prefetch=1,
            grid=(marks // block,),
            in_specs=[
                pl.BlockSpec((block, feats), lambda i, s: (i, 0)),
                pl.BlockSpec((block, classes), lambda i, s: (i, 0)),
                pl.BlockSpec(memory_space=pl.ANY),
            ],
            out_specs=[
                pl.BlockSpec((block, wide), lambda i, s: (i, 0)),
                pl.BlockSpec((block, 2 * classes), lambda i, s: (i, 0)),
                pl.BlockSpec((held_rows, feats), lambda i, s: (0, 0)),
            ],
            scratch_shapes=[pltpu.SemaphoreType.DMA(())],
        ),
        out_shape=[
            pltpu.VMEM((marks, wide), bf16),
            pltpu.VMEM((marks, 2 * classes), bf16),
            pltpu.VMEM((held_rows, feats), f32),
        ],
        compiler_params=pltpu.CompilerParams(vmem_limit_bytes=8 << 20),
        name="prep",
    )(at, landmarks, coefficients, points)


def logits_body(at_ref, p_ref, b_ref, c_ref, *refs, tile, later):
    if later is None:
        hi_ref, lo_ref, far_ref, own_ref, a_ref = refs
    else:
        points_ref, hi_ref, lo_ref, far_ref, own_ref, next_ref, a_ref, sem = refs
        copy = fetched(at_ref, later, points_ref, next_ref, sem)

        @pl.when(pl.program_id(0) == 0)
        def _():
            copy.start()

    rows, feats = p_ref.shape
    marks = b_ref.shape[0]
    unit = math.log2(math.e) / feats
    point = p_ref[...]
    high, low = halves(point)
    a_ref[:, :feats] = high
    a_ref[:, feats : 2 * feats] = high
    a_ref[:, 2 * feats : 3 * feats] = low
    norm = thirds(-unit * jnp.sum(point * point, axis=1, keepdims=True))
    a_ref[:, 3 * feats :] = norm_lanes(rows, [*norm, 1.0, 1.0, 1.0])
    for j in range(marks // tile):
        cols = slice(j * tile, (j + 1) * tile)
        power = lax.dot_general(a_ref[...], b_ref[cols, :], NT, preferred_element_type=f32)
        kernel = jnp.exp2(power)
        high, low = halves(kernel)
        hi_ref[:, cols] = high
        lo_ref[:, cols] = low
    sums = []
    for u in range(2):
        part = slice(u * rows // 2, (u + 1) * rows // 2)
        both = dot(hi_ref[part, :], c_ref[...]) + dot(lo_ref[part, :], c_ref[...])
        sums.append(both[:, : both.shape[1] // 2] + both[:, both.shape[1] // 2 :])

    @pl.when(pl.program_id(0) == 0)
    def _():
        far_ref[...] = jnp.concatenate(sums, axis=0)

    @pl.when(pl.program_id(0) == 1)
    def _():
        own_ref[...] = jnp.concatenate(sums, axis=0)
        if later is not None:
            copy.wait()


def kernel_and_logits(at, held, wide_marks, wide_coefs, points, later, tile=512):
    rows, feats = held.shape
    block = rows // 2
    marks, wide = wide_marks.shape
    classes = wide_coefs.shape[1] // 2
    fixed = pl.Buffered(1)
    fetch = later is not None
    return pl.pallas_call(
        functools.partial(logits_body, tile=tile, later=later),
        grid_spec=pltpu.PrefetchScalarGridSpec(
            num_scalar_prefetch=1,
            grid=(2,),
            in_specs=[
                pl.BlockSpec((block, feats), lambda i, s: (lax.rem(s[1] + 1 + i, 2), 0)),
                pl.BlockSpec((marks, wide), lambda i, s: (0, 0), pipeline_mode=fixed),
                pl.BlockSpec((marks, 2 * classes), lambda i, s: (0, 0), pipeline_mode=fixed),
                *[pl.BlockSpec(memory_space=pl.ANY)] * fetch,
            ],
            out_specs=[
                pl.BlockSpec((block, marks), lambda i, s: (i, 0)),
                pl.BlockSpec((block, marks), lambda i, s: (i, 0)),
                pl.BlockSpec((block, classes), lambda i, s: (0, 0)),
                pl.BlockSpec((block, classes), lambda i, s: (0, 0)),
                *[pl.BlockSpec((rows, feats), lambda i, s: (0, 0))] * fetch,
            ],
            scratch_shapes=[
                pltpu.VMEM((block, wide), bf16),
                *[pltpu.SemaphoreType.DMA(())] * fetch,
            ],
        ),
        out_shape=[
            pltpu.VMEM((rows, marks), bf16),
            pltpu.VMEM((rows, marks), bf16),
            pltpu.VMEM((block, classes), f32),
            pltpu.VMEM((block, classes), f32),
            *[pltpu.VMEM((rows, feats), f32)] * fetch,
        ],
        compiler_params=pltpu.CompilerParams(vmem_limit_bytes=LIMIT_K1 << 20),
        cost_estimate=pl.CostEstimate(
            flops=2 * rows * marks * (wide + 4 * classes),
            bytes_accessed=4 * rows * (feats + marks + classes) + 2 * marks * (wide + 2 * classes),
            transcendentals=rows * marks,
        ),
        name="kernel_and_logits",
    )(at, held, wide_marks, wide_coefs, *[points] * fetch)


def small_kernel(body, at, args, outs, name):
    whole = [pl.BlockSpec(x.shape, lambda i, s: (0, 0)) for x in (*args, *outs)]
    return pl.pallas_call(
        body,
        grid_spec=pltpu.PrefetchScalarGridSpec(
            num_scalar_prefetch=1,
            grid=(1,),
            in_specs=whole[: len(args)],
            out_specs=whole[len(args) :],
        ),
        out_shape=outs,
        compiler_params=pltpu.CompilerParams(vmem_limit_bytes=6 << 20),
        name=name,
    )(at, *args)


def ridge_body(at_ref, c_ref, out_ref):
    out_ref[...] = RIDGE * c_ref[...]


def own_ridge(at, coefficients):
    marks, classes = coefficients.shape
    kept = marks // lax.axis_size(PTS)
    return pl.pallas_call(
        ridge_body,
        grid_spec=pltpu.PrefetchScalarGridSpec(
            num_scalar_prefetch=1,
            grid=(1,),
            in_specs=[pl.BlockSpec((kept, classes), lambda i, s: (s[2], 0))],
            out_specs=pl.BlockSpec((kept, classes), lambda i, s: (0, 0)),
        ),
        out_shape=pltpu.VMEM((kept, classes), f32),
        compiler_params=pltpu.CompilerParams(vmem_limit_bytes=2 << 20),
        name="ridge",
    )(at, pltpu.with_memory_space_constraint(coefficients, pltpu.HBM))


def residual_body(at_ref, labels_ref, a_ref, b_ref, out_ref):
    logits = a_ref[...] + b_ref[...]
    rows, classes = logits.shape
    groups = rows // LANES
    expo = jnp.exp(logits)
    share = expo / jnp.sum(expo, axis=1, keepdims=True)
    base = (at_ref[0] * 2 + at_ref[1]) * groups
    for g in range(groups):
        label = jnp.broadcast_to(labels_ref[pl.ds(base + g, 1), :], (LANES, LANES)).T
        hot = label == lax.broadcasted_iota(jnp.int32, (LANES, classes), 1)
        part = slice(g * LANES, (g + 1) * LANES)
        out_ref[part, :] = share[part, :] - hot.astype(f32)


def terms_body(*refs, sets, tile):
    parts, (*before, out_ref, rt_ref) = refs[: 4 * sets], refs[4 * sets :]
    classes = parts[0].shape[1]
    block = parts[0].shape[0]
    marks = parts[2].shape[1]
    for n in range(sets):
        for h in range(2):
            resid = parts[4 * n + h][...]
            high = resid.astype(bf16).astype(f32)
            rows = slice((2 * n + h) * block, (2 * n + h + 1) * block)
            rt_ref[:classes, rows] = high.T.astype(bf16)
            rt_ref[classes:, rows] = (resid - high).T.astype(bf16)
    for j in range(marks // tile):
        cols = slice(j * tile, (j + 1) * tile)
        both = None
        for n in range(sets):
            left = rt_ref[:, 2 * n * block : 2 * (n + 1) * block]
            for ref in parts[4 * n + 2 : 4 * n + 4]:
                term = dot(left, ref[:, cols])
                both = term if both is None else both + term
        out = (both[:classes, :] + both[classes:, :]).T
        for ref in before:
            out = out + ref[cols, :]
        out_ref[cols, :] = out


def terms(sets, before=None, tile=512):
    args = [x for one in sets for x in one]
    block, classes = args[0].shape
    marks = args[2].shape[1]
    rows = 2 * block * len(sets)
    if before is not None:
        args.append(before)
    return pl.pallas_call(
        functools.partial(terms_body, sets=len(sets), tile=tile),
        in_specs=[pl.BlockSpec(memory_space=pltpu.VMEM)] * len(args),
        out_specs=pl.BlockSpec(memory_space=pltpu.VMEM),
        out_shape=pltpu.VMEM((marks, classes), f32),
        scratch_shapes=[pltpu.VMEM((2 * classes, rows), bf16)],
        compiler_params=pltpu.CompilerParams(vmem_limit_bytes=LIMIT_K2 << 20),
        cost_estimate=pl.CostEstimate(
            flops=8 * rows * marks * classes,
            bytes_accessed=4 * rows * (marks + classes) + 8 * marks * classes,
            transcendentals=0,
        ),
        name="terms",
    )(*args)


def swapped(x):
    return lax.ppermute(x, "core", [(0, 1), (1, 0)])


def summed_share(x, axes):
    devices = lax.axis_size(axes)
    parts = x.reshape(devices, x.shape[0] // devices, x.shape[1])
    return lax.all_to_all(parts, axes, split_axis=0, concat_axis=0, tiled=True).sum(axis=0)


def all_shares(x, axes):
    devices = lax.axis_size(axes)
    copies = jnp.broadcast_to(x, (devices, *x.shape))
    parts = lax.all_to_all(copies, axes, split_axis=0, concat_axis=0, tiled=True)
    return parts.reshape(devices * x.shape[0], x.shape[1])


def along_x(x, shift):
    chips = lax.axis_size("x")
    return lax.ppermute(x, "x", [(i, (i + shift) % chips) for i in range(chips)])


def across_z(x):
    return lax.ppermute(x, "zh", [(0, 1), (1, 0)])


def per_device(points, labels, landmarks, coefficients):
    chips = lax.axis_size("x")
    classes = coefficients.shape[1]
    block = points.shape[0] // (2 * chips)
    at = jnp.stack([lax.axis_index(n) for n in ("x", "core", PTS)]).astype(jnp.int32)
    points, landmarks, first_coefs = (
        pltpu.with_memory_space_constraint(x, pltpu.HBM) for x in (points, landmarks, coefficients)
    )
    at, landmarks = lax.optimization_barrier((at, landmarks))
    wide_marks, wide_coefs, held = prep(at, 2, landmarks, first_coefs, points, 2 * block)
    made, mine, arrived, sums = {}, {}, {}, []
    for shift, later, ready in ((2, 1, ()), (1, 3, (2,)), (3, 0, (1, 3)), (0, None, ())):
        hi, lo, far, own, *after = kernel_and_logits(at, held, wide_marks, wide_coefs, points, later)
        held = after[0] if after else None
        made[shift] = hi, lo
        mine[shift], arrived[shift] = own, swapped(far)
        both = [mine[n] + arrived[n] for n in ready]
        if both:
            at, both = lax.optimization_barrier((at, both))
        sums += [along_x(x, n) for x, n in zip(both, ready)]
    logits = mine[0] + arrived[0] + sums[0] + sums[1] + sums[2]
    full = jax.ShapeDtypeStruct((block, classes), f32)
    by_group = labels.reshape(-1, LANES)
    (own,) = small_kernel(residual_body, at, [by_group, logits, across_z(logits)], [full], "residual")
    near = {3: along_x(own, 1), 1: along_x(own, 3)}
    local = terms([(swapped(own), own, *made[0])])
    at, local = lax.optimization_barrier((at, local))
    ridge = own_ridge(at, coefficients)
    local, near, ridge = lax.optimization_barrier((local, near, ridge))
    front, back = along_x(near[3][: block // 2], 1), along_x(near[1][block // 2 :], 3)
    local = terms([(swapped(near[n]), near[n], *made[n]) for n in (3, 1)], local)
    local, front, back = lax.optimization_barrier((local, front, back))
    last = jnp.concatenate([front, back], axis=0)
    local = terms([(swapped(last), last, *made[2])], local)
    total_points = labels.shape[0] * lax.axis_size(PTS)
    share = summed_share(local, PTS)
    return all_shares(share * (LOSS_SCALE / total_points) + ridge, PTS)


def solution(mesh):
    fine = Mesh(mesh.devices.reshape(4, 2, 2, 4, 2), AXES)
    in_specs = (P(PTS, None), P(PTS), P(LMK, None), P(LMK, None))
    return jax.shard_map(
        per_device, mesh=fine, in_specs=in_specs, out_specs=P(LMK, None), check_vma=False
    )
```

```python
import functools
import math

import jax
import jax.numpy as jnp
from jax import lax
from jax.experimental import pallas as pl
from jax.experimental.pallas import tpu as pltpu
from jax.sharding import Mesh
from jax.sharding import PartitionSpec as P

LOSS_SCALE = 8192.0
RIDGE = 0.5
LIMIT_K1, LIMIT_K2 = 8, 6
LANES = 128
AXES = ("y", "zl", "zh", "x", "core")
PTS = ("y", "zl")
LMK = ("zh", "x", "core")
NT = (((1,), (1,)), ((), ()))
f32, bf16 = jnp.float32, jnp.bfloat16


def dot(a, b):
    return jnp.dot(a, b, preferred_element_type=f32)


def halves(x):
    high = x.astype(bf16)
    return high, (x - high.astype(f32)).astype(bf16)


def thirds(x):
    a = x.astype(bf16).astype(f32)
    b = (x - a).astype(bf16).astype(f32)
    return a, b, x - a - b


def norm_lanes(rows, columns):
    lane = lax.broadcasted_iota(jnp.int32, (rows, LANES), 1)
    out = jnp.zeros((rows, LANES), f32)
    for i, column in enumerate(columns):
        out = jnp.where(lane == i, column, out)
    return out.astype(bf16)


def fetched(at_ref, shift, points_ref, next_ref, sem):
    rows = next_ref.shape[0]
    chips = points_ref.shape[0] // rows
    first = pl.multiple_of(lax.rem(at_ref[0] + shift, chips) * rows, rows)
    return pltpu.make_async_copy(points_ref.at[pl.ds(first, rows), :], next_ref, sem)


def prep_body(at_ref, l_ref, c_ref, points_ref, b_ref, cc_ref, next_ref, sem, *, shift):
    copy = fetched(at_ref, shift, points_ref, next_ref, sem)

    @pl.when(pl.program_id(0) == 0)
    def _():
        copy.start()

    rows, feats = l_ref.shape
    unit = math.log2(math.e) / feats
    mark = l_ref[...]
    high, low = halves(mark * (2.0 * unit))
    b_ref[:, :feats] = high
    b_ref[:, feats : 2 * feats] = low
    b_ref[:, 2 * feats : 3 * feats] = high
    norm = thirds(-unit * jnp.sum(mark * mark, axis=1, keepdims=True))
    b_ref[:, 3 * feats :] = norm_lanes(rows, [1.0, 1.0, 1.0, *norm])
    high, low = halves(c_ref[...])
    cc_ref[:, : high.shape[1]] = high
    cc_ref[:, high.shape[1] :] = low

    @pl.when(pl.program_id(0) == pl.num_programs(0) - 1)
    def _():
        copy.wait()


def prep(at, shift, landmarks, coefficients, points, held_rows, block=1024):
    marks, feats = landmarks.shape
    classes = coefficients.shape[1]
    wide = 3 * feats + LANES
    return pl.pallas_call(
        functools.partial(prep_body, shift=shift),
        grid_spec=pltpu.PrefetchScalarGridSpec(
            num_scalar_prefetch=1,
            grid=(marks // block,),
            in_specs=[
                pl.BlockSpec((block, feats), lambda i, s: (i, 0)),
                pl.BlockSpec((block, classes), lambda i, s: (i, 0)),
                pl.BlockSpec(memory_space=pl.ANY),
            ],
            out_specs=[
                pl.BlockSpec((block, wide), lambda i, s: (i, 0)),
                pl.BlockSpec((block, 2 * classes), lambda i, s: (i, 0)),
                pl.BlockSpec((held_rows, feats), lambda i, s: (0, 0)),
            ],
            scratch_shapes=[pltpu.SemaphoreType.DMA(())],
        ),
        out_shape=[
            pltpu.VMEM((marks, wide), bf16),
            pltpu.VMEM((marks, 2 * classes), bf16),
            pltpu.VMEM((held_rows, feats), f32),
        ],
        compiler_params=pltpu.CompilerParams(vmem_limit_bytes=12 << 20),
        name="prep",
    )(at, landmarks, coefficients, points)


def logits_body(at_ref, p_ref, b_ref, c_ref, *refs, tile, later):
    if later is None:
        hi_ref, lo_ref, far_ref, own_ref, a_ref = refs
    else:
        points_ref, hi_ref, lo_ref, far_ref, own_ref, next_ref, a_ref, sem = refs
        copy = fetched(at_ref, later, points_ref, next_ref, sem)

        @pl.when(pl.program_id(0) == 0)
        def _():
            copy.start()

    rows, feats = p_ref.shape
    marks = b_ref.shape[0]
    unit = math.log2(math.e) / feats
    point = p_ref[...]
    high, low = halves(point)
    a_ref[:, :feats] = high
    a_ref[:, feats : 2 * feats] = high
    a_ref[:, 2 * feats : 3 * feats] = low
    norm = thirds(-unit * jnp.sum(point * point, axis=1, keepdims=True))
    a_ref[:, 3 * feats :] = norm_lanes(rows, [*norm, 1.0, 1.0, 1.0])
    for j in range(marks // tile):
        cols = slice(j * tile, (j + 1) * tile)
        power = lax.dot_general(a_ref[...], b_ref[cols, :], NT, preferred_element_type=f32)
        kernel = jnp.exp2(power)
        high, low = halves(kernel)
        hi_ref[:, cols] = high
        lo_ref[:, cols] = low
    sums = []
    for u in range(2):
        part = slice(u * rows // 2, (u + 1) * rows // 2)
        both = dot(hi_ref[part, :], c_ref[...]) + dot(lo_ref[part, :], c_ref[...])
        sums.append(both[:, : both.shape[1] // 2] + both[:, both.shape[1] // 2 :])

    @pl.when(pl.program_id(0) == 0)
    def _():
        far_ref[...] = jnp.concatenate(sums, axis=0)

    @pl.when(pl.program_id(0) == 1)
    def _():
        own_ref[...] = jnp.concatenate(sums, axis=0)
        if later is not None:
            copy.wait()


def kernel_and_logits(at, held, wide_marks, wide_coefs, points, later, tile=512):
    rows, feats = held.shape
    block = rows // 2
    marks, wide = wide_marks.shape
    classes = wide_coefs.shape[1] // 2
    fixed = pl.Buffered(1)
    fetch = later is not None
    return pl.pallas_call(
        functools.partial(logits_body, tile=tile, later=later),
        grid_spec=pltpu.PrefetchScalarGridSpec(
            num_scalar_prefetch=1,
            grid=(2,),
            in_specs=[
                pl.BlockSpec((block, feats), lambda i, s: (lax.rem(s[1] + 1 + i, 2), 0)),
                pl.BlockSpec((marks, wide), lambda i, s: (0, 0), pipeline_mode=fixed),
                pl.BlockSpec((marks, 2 * classes), lambda i, s: (0, 0), pipeline_mode=fixed),
                *[pl.BlockSpec(memory_space=pl.ANY)] * fetch,
            ],
            out_specs=[
                pl.BlockSpec((block, marks), lambda i, s: (i, 0)),
                pl.BlockSpec((block, marks), lambda i, s: (i, 0)),
                pl.BlockSpec((block, classes), lambda i, s: (0, 0)),
                pl.BlockSpec((block, classes), lambda i, s: (0, 0)),
                *[pl.BlockSpec((rows, feats), lambda i, s: (0, 0))] * fetch,
            ],
            scratch_shapes=[
                pltpu.VMEM((block, wide), bf16),
                *[pltpu.SemaphoreType.DMA(())] * fetch,
            ],
        ),
        out_shape=[
            pltpu.VMEM((rows, marks), bf16),
            pltpu.VMEM((rows, marks), bf16),
            pltpu.VMEM((block, classes), f32),
            pltpu.VMEM((block, classes), f32),
            *[pltpu.VMEM((rows, feats), f32)] * fetch,
        ],
        compiler_params=pltpu.CompilerParams(vmem_limit_bytes=LIMIT_K1 << 20),
        cost_estimate=pl.CostEstimate(
            flops=2 * rows * marks * (wide + 4 * classes),
            bytes_accessed=4 * rows * (feats + marks + classes) + 2 * marks * (wide + 2 * classes),
            transcendentals=rows * marks,
        ),
        name="kernel_and_logits",
    )(at, held, wide_marks, wide_coefs, *[points] * fetch)


def small_kernel(body, at, args, outs, name):
    whole = [pl.BlockSpec(x.shape, lambda i, s: (0, 0)) for x in (*args, *outs)]
    return pl.pallas_call(
        body,
        grid_spec=pltpu.PrefetchScalarGridSpec(
            num_scalar_prefetch=1,
            grid=(1,),
            in_specs=whole[: len(args)],
            out_specs=whole[len(args) :],
        ),
        out_shape=outs,
        compiler_params=pltpu.CompilerParams(vmem_limit_bytes=6 << 20),
        name=name,
    )(at, *args)


def ridge_body(at_ref, c_ref, out_ref):
    out_ref[...] = RIDGE * c_ref[...]


def own_ridge(at, coefficients):
    marks, classes = coefficients.shape
    kept = marks // lax.axis_size(PTS)
    return pl.pallas_call(
        ridge_body,
        grid_spec=pltpu.PrefetchScalarGridSpec(
            num_scalar_prefetch=1,
            grid=(1,),
            in_specs=[pl.BlockSpec((kept, classes), lambda i, s: (s[2], 0))],
            out_specs=pl.BlockSpec((kept, classes), lambda i, s: (0, 0)),
        ),
        out_shape=pltpu.VMEM((kept, classes), f32),
        compiler_params=pltpu.CompilerParams(vmem_limit_bytes=2 << 20),
        name="ridge",
    )(at, pltpu.with_memory_space_constraint(coefficients, pltpu.HBM))


def residual_body(at_ref, labels_ref, a_ref, b_ref, out_ref):
    logits = a_ref[...] + b_ref[...]
    rows, classes = logits.shape
    groups = rows // LANES
    expo = jnp.exp(logits)
    share = expo / jnp.sum(expo, axis=1, keepdims=True)
    base = (at_ref[0] * 2 + at_ref[1]) * groups
    for g in range(groups):
        label = jnp.broadcast_to(labels_ref[pl.ds(base + g, 1), :], (LANES, LANES)).T
        hot = label == lax.broadcasted_iota(jnp.int32, (LANES, classes), 1)
        part = slice(g * LANES, (g + 1) * LANES)
        out_ref[part, :] = share[part, :] - hot.astype(f32)


def terms_body(*refs, sets, tile):
    parts, (*before, out_ref, rt_ref) = refs[: 4 * sets], refs[4 * sets :]
    classes = parts[0].shape[1]
    block = parts[0].shape[0]
    marks = parts[2].shape[1]
    for n in range(sets):
        for h in range(2):
            resid = parts[4 * n + h][...]
            high = resid.astype(bf16).astype(f32)
            rows = slice((2 * n + h) * block, (2 * n + h + 1) * block)
            rt_ref[:classes, rows] = high.T.astype(bf16)
            rt_ref[classes:, rows] = (resid - high).T.astype(bf16)
    for j in range(marks // tile):
        cols = slice(j * tile, (j + 1) * tile)
        both, small = None, None
        for n in range(sets):
            rows = slice(2 * n * block, 2 * (n + 1) * block)
            term = dot(rt_ref[:, rows], parts[4 * n + 2][:, cols])
            both = term if both is None else both + term
            term = dot(rt_ref[:classes, rows], parts[4 * n + 3][:, cols])
            small = term if small is None else small + term
        out = (both[:classes, :] + both[classes:, :] + small).T
        for ref in before:
            out = out + ref[cols, :]
        out_ref[cols, :] = out


def terms(sets, before=None, tile=512):
    args = [x for one in sets for x in one]
    block, classes = args[0].shape
    marks = args[2].shape[1]
    rows = 2 * block * len(sets)
    if before is not None:
        args.append(before)
    return pl.pallas_call(
        functools.partial(terms_body, sets=len(sets), tile=tile),
        in_specs=[pl.BlockSpec(memory_space=pltpu.VMEM)] * len(args),
        out_specs=pl.BlockSpec(memory_space=pltpu.VMEM),
        out_shape=pltpu.VMEM((marks, classes), f32),
        scratch_shapes=[pltpu.VMEM((2 * classes, rows), bf16)],
        compiler_params=pltpu.CompilerParams(vmem_limit_bytes=LIMIT_K2 << 20),
        cost_estimate=pl.CostEstimate(
            flops=8 * rows * marks * classes,
            bytes_accessed=4 * rows * (marks + classes) + 8 * marks * classes,
            transcendentals=0,
        ),
        name="terms",
    )(*args)


def swapped(x):
    return lax.ppermute(x, "core", [(0, 1), (1, 0)])


def summed_share(x, axes):
    devices = lax.axis_size(axes)
    parts = x.reshape(devices, x.shape[0] // devices, x.shape[1])
    return lax.all_to_all(parts, axes, split_axis=0, concat_axis=0, tiled=True).sum(axis=0)


def all_shares(x, axes):
    devices = lax.axis_size(axes)
    copies = jnp.broadcast_to(x, (devices, *x.shape))
    parts = lax.all_to_all(copies, axes, split_axis=0, concat_axis=0, tiled=True)
    return parts.reshape(devices * x.shape[0], x.shape[1])


def along_x(x, shift):
    chips = lax.axis_size("x")
    return lax.ppermute(x, "x", [(i, (i + shift) % chips) for i in range(chips)])


def across_z(x):
    return lax.ppermute(x, "zh", [(0, 1), (1, 0)])


def per_device(points, labels, landmarks, coefficients):
    chips = lax.axis_size("x")
    classes = coefficients.shape[1]
    block = points.shape[0] // (2 * chips)
    at = jnp.stack([lax.axis_index(n) for n in ("x", "core", PTS)]).astype(jnp.int32)
    points, landmarks, first_coefs = (
        pltpu.with_memory_space_constraint(x, pltpu.HBM) for x in (points, landmarks, coefficients)
    )
    at, landmarks = lax.optimization_barrier((at, landmarks))
    wide_marks, wide_coefs, held = prep(at, 2, landmarks, first_coefs, points, 2 * block)
    made, mine, arrived, sums = {}, {}, {}, []
    for shift, later, ready in ((2, 1, ()), (1, 3, (2,)), (3, 0, (1, 3)), (0, None, ())):
        hi, lo, far, own, *after = kernel_and_logits(at, held, wide_marks, wide_coefs, points, later)
        held = after[0] if after else None
        made[shift] = hi, lo
        mine[shift], arrived[shift] = own, swapped(far)
        both = [mine[n] + arrived[n] for n in ready]
        if both:
            at, both = lax.optimization_barrier((at, both))
        sums += [along_x(x, n) for x, n in zip(both, ready)]
    logits = mine[0] + arrived[0] + sums[0] + sums[1] + sums[2]
    full = jax.ShapeDtypeStruct((block, classes), f32)
    by_group = labels.reshape(-1, LANES)
    (own,) = small_kernel(residual_body, at, [by_group, logits, across_z(logits)], [full], "residual")
    near = {3: along_x(own, 1), 1: along_x(own, 3)}
    local = terms([(swapped(own), own, *made[0])])
    at, local = lax.optimization_barrier((at, local))
    ridge = own_ridge(at, coefficients)
    local, near, ridge = lax.optimization_barrier((local, near, ridge))
    front, back = along_x(near[3][: block // 2], 1), along_x(near[1][block // 2 :], 3)
    local = terms([(swapped(near[n]), near[n], *made[n]) for n in (3, 1)], local)
    local, front, back = lax.optimization_barrier((local, front, back))
    last = jnp.concatenate([front, back], axis=0)
    local = terms([(swapped(last), last, *made[2])], local)
    total_points = labels.shape[0] * lax.axis_size(PTS)
    share = summed_share(local, PTS)
    return all_shares(share * (LOSS_SCALE / total_points) + ridge, PTS)


def solution(mesh):
    fine = Mesh(mesh.devices.reshape(4, 2, 2, 4, 2), AXES)
    in_specs = (P(PTS, None), P(PTS), P(LMK, None), P(LMK, None))
    return jax.shard_map(
        per_device, mesh=fine, in_specs=in_specs, out_specs=P(LMK, None), check_vma=False
    )
```

```python
import functools
import math

import jax
import jax.numpy as jnp
from jax import lax
from jax.experimental import pallas as pl
from jax.experimental.pallas import tpu as pltpu
from jax.sharding import Mesh
from jax.sharding import PartitionSpec as P

LOSS_SCALE = 8192.0
RIDGE = 0.5
LIMIT_K1, LIMIT_K2 = 8, 6
LANES = 128
AXES = ("y", "zl", "zh", "x", "core")
PTS = ("y", "zl")
LMK = ("zh", "x", "core")
NT = (((1,), (1,)), ((), ()))
f32, bf16 = jnp.float32, jnp.bfloat16


def dot(a, b):
    return jnp.dot(a, b, preferred_element_type=f32)


def halves(x):
    high = x.astype(bf16)
    return high, (x - high.astype(f32)).astype(bf16)


def thirds(x):
    a = x.astype(bf16).astype(f32)
    b = (x - a).astype(bf16).astype(f32)
    return a, b, x - a - b


def norm_lanes(rows, columns):
    lane = lax.broadcasted_iota(jnp.int32, (rows, LANES), 1)
    out = jnp.zeros((rows, LANES), f32)
    for i, column in enumerate(columns):
        out = jnp.where(lane == i, column, out)
    return out.astype(bf16)


def fetched(at_ref, shift, points_ref, next_ref, sem):
    rows = next_ref.shape[0]
    chips = points_ref.shape[0] // rows
    first = pl.multiple_of(lax.rem(at_ref[0] + shift, chips) * rows, rows)
    return pltpu.make_async_copy(points_ref.at[pl.ds(first, rows), :], next_ref, sem)


def prep_body(at_ref, l_ref, c_ref, points_ref, b_ref, cc_ref, next_ref, sem, *, shift):
    copy = fetched(at_ref, shift, points_ref, next_ref, sem)

    @pl.when(pl.program_id(0) == 0)
    def _():
        copy.start()

    rows, feats = l_ref.shape
    unit = math.log2(math.e) / feats
    mark = l_ref[...]
    high, low = halves(mark * (2.0 * unit))
    b_ref[:, :feats] = high
    b_ref[:, feats : 2 * feats] = low
    b_ref[:, 2 * feats : 3 * feats] = high
    norm = thirds(-unit * jnp.sum(mark * mark, axis=1, keepdims=True))
    b_ref[:, 3 * feats :] = norm_lanes(rows, [1.0, 1.0, 1.0, *norm])
    high, low = halves(c_ref[...])
    cc_ref[:, : high.shape[1]] = high
    cc_ref[:, high.shape[1] :] = low

    @pl.when(pl.program_id(0) == pl.num_programs(0) - 1)
    def _():
        copy.wait()


def prep(at, shift, landmarks, coefficients, points, held_rows, block=1024):
    marks, feats = landmarks.shape
    classes = coefficients.shape[1]
    wide = 3 * feats + LANES
    return pl.pallas_call(
        functools.partial(prep_body, shift=shift),
        grid_spec=pltpu.PrefetchScalarGridSpec(
            num_scalar_prefetch=1,
            grid=(marks // block,),
            in_specs=[
                pl.BlockSpec((block, feats), lambda i, s: (i, 0)),
                pl.BlockSpec((block, classes), lambda i, s: (i, 0)),
                pl.BlockSpec(memory_space=pl.ANY),
            ],
            out_specs=[
                pl.BlockSpec((block, wide), lambda i, s: (i, 0)),
                pl.BlockSpec((block, 2 * classes), lambda i, s: (i, 0)),
                pl.BlockSpec((held_rows, feats), lambda i, s: (0, 0)),
            ],
            scratch_shapes=[pltpu.SemaphoreType.DMA(())],
        ),
        out_shape=[
            pltpu.VMEM((marks, wide), bf16),
            pltpu.VMEM((marks, 2 * classes), bf16),
            pltpu.VMEM((held_rows, feats), f32),
        ],
        compiler_params=pltpu.CompilerParams(vmem_limit_bytes=12 << 20),
        name="prep",
    )(at, landmarks, coefficients, points)


def logits_body(at_ref, p_ref, b_ref, c_ref, *refs, tile, later):
    if later is None:
        hi_ref, lo_ref, far_ref, own_ref, a_ref = refs
    else:
        points_ref, hi_ref, lo_ref, far_ref, own_ref, next_ref, a_ref, sem = refs
        copy = fetched(at_ref, later, points_ref, next_ref, sem)

        @pl.when(pl.program_id(0) == 0)
        def _():
            copy.start()

    rows, feats = p_ref.shape
    marks = b_ref.shape[0]
    unit = math.log2(math.e) / feats
    point = p_ref[...]
    high, low = halves(point)
    a_ref[:, :feats] = high
    a_ref[:, feats : 2 * feats] = high
    a_ref[:, 2 * feats : 3 * feats] = low
    norm = thirds(-unit * jnp.sum(point * point, axis=1, keepdims=True))
    a_ref[:, 3 * feats :] = norm_lanes(rows, [*norm, 1.0, 1.0, 1.0])
    for j in range(marks // tile):
        cols = slice(j * tile, (j + 1) * tile)
        power = lax.dot_general(a_ref[...], b_ref[cols, :], NT, preferred_element_type=f32)
        kernel = jnp.exp2(power)
        high, low = halves(kernel)
        hi_ref[:, cols] = high
        lo_ref[:, cols] = low
    sums = []
    for u in range(2):
        part = slice(u * rows // 2, (u + 1) * rows // 2)
        both = dot(hi_ref[part, :], c_ref[...]) + dot(lo_ref[part, :], c_ref[...])
        sums.append(both[:, : both.shape[1] // 2] + both[:, both.shape[1] // 2 :])

    @pl.when(pl.program_id(0) == 0)
    def _():
        far_ref[...] = jnp.concatenate(sums, axis=0)

    @pl.when(pl.program_id(0) == 1)
    def _():
        own_ref[...] = jnp.concatenate(sums, axis=0)
        if later is not None:
            copy.wait()


def kernel_and_logits(at, held, wide_marks, wide_coefs, points, later, tile=512):
    rows, feats = held.shape
    block = rows // 2
    marks, wide = wide_marks.shape
    classes = wide_coefs.shape[1] // 2
    fixed = pl.Buffered(1)
    fetch = later is not None
    return pl.pallas_call(
        functools.partial(logits_body, tile=tile, later=later),
        grid_spec=pltpu.PrefetchScalarGridSpec(
            num_scalar_prefetch=1,
            grid=(2,),
            in_specs=[
                pl.BlockSpec((block, feats), lambda i, s: (lax.rem(s[1] + 1 + i, 2), 0)),
                pl.BlockSpec((marks, wide), lambda i, s: (0, 0), pipeline_mode=fixed),
                pl.BlockSpec((marks, 2 * classes), lambda i, s: (0, 0), pipeline_mode=fixed),
                *[pl.BlockSpec(memory_space=pl.ANY)] * fetch,
            ],
            out_specs=[
                pl.BlockSpec((block, marks), lambda i, s: (i, 0)),
                pl.BlockSpec((block, marks), lambda i, s: (i, 0)),
                pl.BlockSpec((block, classes), lambda i, s: (0, 0)),
                pl.BlockSpec((block, classes), lambda i, s: (0, 0)),
                *[pl.BlockSpec((rows, feats), lambda i, s: (0, 0))] * fetch,
            ],
            scratch_shapes=[
                pltpu.VMEM((block, wide), bf16),
                *[pltpu.SemaphoreType.DMA(())] * fetch,
            ],
        ),
        out_shape=[
            pltpu.VMEM((rows, marks), bf16),
            pltpu.VMEM((rows, marks), bf16),
            pltpu.VMEM((block, classes), f32),
            pltpu.VMEM((block, classes), f32),
            *[pltpu.VMEM((rows, feats), f32)] * fetch,
        ],
        compiler_params=pltpu.CompilerParams(vmem_limit_bytes=LIMIT_K1 << 20),
        cost_estimate=pl.CostEstimate(
            flops=2 * rows * marks * (wide + 4 * classes),
            bytes_accessed=4 * rows * (feats + marks + classes) + 2 * marks * (wide + 2 * classes),
            transcendentals=rows * marks,
        ),
        name="kernel_and_logits",
    )(at, held, wide_marks, wide_coefs, *[points] * fetch)


def block_and_logits(at, which, held, wide_marks, wide_coefs, tile=512):
    feats = held.shape[1]
    block = held.shape[0] // 2
    marks, wide = wide_marks.shape
    classes = wide_coefs.shape[1] // 2
    fixed = pl.Buffered(1)

    def body(at_ref, p_ref, b_ref, c_ref, hi_ref, lo_ref, out_ref, a_ref):
        logits_body(
            at_ref, p_ref, b_ref, c_ref, hi_ref, lo_ref, out_ref, out_ref, a_ref, tile=tile, later=None
        )

    return pl.pallas_call(
        body,
        grid_spec=pltpu.PrefetchScalarGridSpec(
            num_scalar_prefetch=1,
            grid=(1,),
            in_specs=[
                pl.BlockSpec((block, feats), lambda i, s: (lax.rem(s[1] + 1 + which, 2), 0)),
                pl.BlockSpec((marks, wide), lambda i, s: (0, 0), pipeline_mode=fixed),
                pl.BlockSpec((marks, 2 * classes), lambda i, s: (0, 0), pipeline_mode=fixed),
            ],
            out_specs=[
                pl.BlockSpec((block, marks), lambda i, s: (0, 0)),
                pl.BlockSpec((block, marks), lambda i, s: (0, 0)),
                pl.BlockSpec((block, classes), lambda i, s: (0, 0)),
            ],
            scratch_shapes=[pltpu.VMEM((block, wide), bf16)],
        ),
        out_shape=[
            pltpu.VMEM((block, marks), bf16),
            pltpu.VMEM((block, marks), bf16),
            pltpu.VMEM((block, classes), f32),
        ],
        compiler_params=pltpu.CompilerParams(vmem_limit_bytes=LIMIT_K1 << 20),
        cost_estimate=pl.CostEstimate(
            flops=2 * block * classes, bytes_accessed=4 * block * classes, transcendentals=0
        ),
        name="block_and_logits",
    )(at, held, wide_marks, wide_coefs)


def small_kernel(body, at, args, outs, name):
    whole = [pl.BlockSpec(x.shape, lambda i, s: (0, 0)) for x in (*args, *outs)]
    return pl.pallas_call(
        body,
        grid_spec=pltpu.PrefetchScalarGridSpec(
            num_scalar_prefetch=1,
            grid=(1,),
            in_specs=whole[: len(args)],
            out_specs=whole[len(args) :],
        ),
        out_shape=outs,
        compiler_params=pltpu.CompilerParams(vmem_limit_bytes=6 << 20),
        name=name,
    )(at, *args)


def ridge_body(at_ref, c_ref, out_ref):
    out_ref[...] = RIDGE * c_ref[...]


def own_ridge(at, coefficients):
    marks, classes = coefficients.shape
    kept = marks // lax.axis_size(PTS)
    return pl.pallas_call(
        ridge_body,
        grid_spec=pltpu.PrefetchScalarGridSpec(
            num_scalar_prefetch=1,
            grid=(1,),
            in_specs=[pl.BlockSpec((kept, classes), lambda i, s: (s[2], 0))],
            out_specs=pl.BlockSpec((kept, classes), lambda i, s: (0, 0)),
        ),
        out_shape=pltpu.VMEM((kept, classes), f32),
        compiler_params=pltpu.CompilerParams(vmem_limit_bytes=2 << 20),
        name="ridge",
    )(at, pltpu.with_memory_space_constraint(coefficients, pltpu.HBM))


def residual_body(at_ref, labels_ref, a_ref, b_ref, out_ref):
    logits = a_ref[...] + b_ref[...]
    rows, classes = logits.shape
    groups = rows // LANES
    expo = jnp.exp(logits)
    share = expo / jnp.sum(expo, axis=1, keepdims=True)
    base = (at_ref[0] * 2 + at_ref[1]) * groups
    for g in range(groups):
        label = jnp.broadcast_to(labels_ref[pl.ds(base + g, 1), :], (LANES, LANES)).T
        hot = label == lax.broadcasted_iota(jnp.int32, (LANES, classes), 1)
        part = slice(g * LANES, (g + 1) * LANES)
        out_ref[part, :] = share[part, :] - hot.astype(f32)


def terms_body(*refs, sets, pieces, tile):
    width = pieces + 2
    parts, (*before, out_ref, rt_ref) = refs[: width * sets], refs[width * sets :]
    block, classes = parts[0].shape
    marks = parts[pieces].shape[1]
    for n in range(sets):
        for h in range(pieces):
            resid = parts[width * n + h][...]
            high = resid.astype(bf16).astype(f32)
            rows = slice((pieces * n + h) * block, (pieces * n + h + 1) * block)
            rt_ref[:classes, rows] = high.T.astype(bf16)
            rt_ref[classes:, rows] = (resid - high).T.astype(bf16)
    for j in range(marks // tile):
        cols = slice(j * tile, (j + 1) * tile)
        both, small = None, None
        for n in range(sets):
            rows = slice(pieces * n * block, pieces * (n + 1) * block)
            term = dot(rt_ref[:, rows], parts[width * n + pieces][:, cols])
            both = term if both is None else both + term
            term = dot(rt_ref[:classes, rows], parts[width * n + pieces + 1][:, cols])
            small = term if small is None else small + term
        out = (both[:classes, :] + both[classes:, :] + small).T
        for ref in before:
            out = out + ref[cols, :]
        out_ref[cols, :] = out


def terms(sets, before=None, tile=512):
    args = [x for one in sets for x in one]
    block, classes = args[0].shape
    pieces = len(sets[0]) - 2
    marks = args[pieces].shape[1]
    rows = pieces * block * len(sets)
    if before is not None:
        args.append(before)
    return pl.pallas_call(
        functools.partial(terms_body, sets=len(sets), pieces=pieces, tile=tile),
        in_specs=[pl.BlockSpec(memory_space=pltpu.VMEM)] * len(args),
        out_specs=pl.BlockSpec(memory_space=pltpu.VMEM),
        out_shape=pltpu.VMEM((marks, classes), f32),
        scratch_shapes=[pltpu.VMEM((2 * classes, rows), bf16)],
        compiler_params=pltpu.CompilerParams(vmem_limit_bytes=LIMIT_K2 << 20),
        cost_estimate=pl.CostEstimate(
            flops=8 * rows * marks * classes,
            bytes_accessed=4 * rows * (marks + classes) + 8 * marks * classes,
            transcendentals=0,
        ),
        name="terms",
    )(*args)


def swapped(x):
    return lax.ppermute(x, "core", [(0, 1), (1, 0)])


def summed_share(x, axes):
    devices = lax.axis_size(axes)
    parts = x.reshape(devices, x.shape[0] // devices, x.shape[1])
    return lax.all_to_all(parts, axes, split_axis=0, concat_axis=0, tiled=True).sum(axis=0)


def all_shares(x, axes):
    devices = lax.axis_size(axes)
    copies = jnp.broadcast_to(x, (devices, *x.shape))
    parts = lax.all_to_all(copies, axes, split_axis=0, concat_axis=0, tiled=True)
    return parts.reshape(devices * x.shape[0], x.shape[1])


def along_x(x, shift):
    chips = lax.axis_size("x")
    return lax.ppermute(x, "x", [(i, (i + shift) % chips) for i in range(chips)])


def across_z(x):
    return lax.ppermute(x, "zh", [(0, 1), (1, 0)])


def per_device(points, labels, landmarks, coefficients):
    chips = lax.axis_size("x")
    classes = coefficients.shape[1]
    block = points.shape[0] // (2 * chips)
    at = jnp.stack([lax.axis_index(n) for n in ("x", "core", PTS)]).astype(jnp.int32)
    points, landmarks, first_coefs = (
        pltpu.with_memory_space_constraint(x, pltpu.HBM) for x in (points, landmarks, coefficients)
    )
    at, landmarks = lax.optimization_barrier((at, landmarks))
    wide_marks, wide_coefs, held = prep(at, 2, landmarks, first_coefs, points, 2 * block)
    made, mine, arrived, sums = {}, {}, {}, []
    for shift, later, ready in ((2, 1, ()), (1, 3, (2,)), (3, 0, (1, 3))):
        hi, lo, far, own, *after = kernel_and_logits(at, held, wide_marks, wide_coefs, points, later)
        held = after[0]
        made[shift] = hi, lo
        mine[shift], arrived[shift] = own, swapped(far)
        both = [mine[n] + arrived[n] for n in ready]
        if both:
            at, both = lax.optimization_barrier((at, both))
        sums += [along_x(x, n) for x, n in zip(both, ready)]
    *far_made, far = block_and_logits(at, 0, held, wide_marks, wide_coefs)
    over = swapped(far)
    at, far = lax.optimization_barrier((at, far))
    *own_made, own = block_and_logits(at, 1, held, wide_marks, wide_coefs)
    logits = own + over + sums[0] + sums[1] + sums[2]
    full = jax.ShapeDtypeStruct((block, classes), f32)
    by_group = labels.reshape(-1, LANES)
    (own,) = small_kernel(residual_body, at, [by_group, logits, across_z(logits)], [full], "residual")
    near = {3: along_x(own, 1), 1: along_x(own, 3)}
    local = terms([(swapped(own), *far_made), (own, *own_made)])
    at, local = lax.optimization_barrier((at, local))
    ridge = own_ridge(at, coefficients)
    local, near, ridge = lax.optimization_barrier((local, near, ridge))
    front, back = along_x(near[3][: block // 2], 1), along_x(near[1][block // 2 :], 3)
    local = terms([(swapped(near[n]), near[n], *made[n]) for n in (3, 1)], local)
    local, front, back = lax.optimization_barrier((local, front, back))
    last = jnp.concatenate([front, back], axis=0)
    local = terms([(swapped(last), last, *made[2])], local)
    total_points = labels.shape[0] * lax.axis_size(PTS)
    share = summed_share(local, PTS)
    return all_shares(share * (LOSS_SCALE / total_points) + ridge, PTS)


def solution(mesh):
    fine = Mesh(mesh.devices.reshape(4, 2, 2, 4, 2), AXES)
    in_specs = (P(PTS, None), P(PTS), P(LMK, None), P(LMK, None))
    return jax.shard_map(
        per_device, mesh=fine, in_specs=in_specs, out_specs=P(LMK, None), check_vma=False
    )
```

```python
import functools
import math

import jax
import jax.numpy as jnp
from jax import lax
from jax.experimental import pallas as pl
from jax.experimental.pallas import tpu as pltpu
from jax.sharding import Mesh
from jax.sharding import PartitionSpec as P

LOSS_SCALE = 8192.0
RIDGE = 0.5
LIMIT_K1, LIMIT_K2 = 8, 6
LANES = 128
AXES = ("y", "zl", "zh", "x", "core")
PTS = ("y", "zl")
LMK = ("zh", "x", "core")
NT = (((1,), (1,)), ((), ()))
f32, bf16 = jnp.float32, jnp.bfloat16


def dot(a, b):
    return jnp.dot(a, b, preferred_element_type=f32)


def halves(x):
    high = x.astype(bf16)
    return high, (x - high.astype(f32)).astype(bf16)


def thirds(x):
    a = x.astype(bf16).astype(f32)
    b = (x - a).astype(bf16).astype(f32)
    return a, b, x - a - b


def norm_lanes(rows, columns):
    lane = lax.broadcasted_iota(jnp.int32, (rows, LANES), 1)
    out = jnp.zeros((rows, LANES), f32)
    for i, column in enumerate(columns):
        out = jnp.where(lane == i, column, out)
    return out.astype(bf16)


def fetched(at_ref, shift, points_ref, next_ref, sem):
    rows = next_ref.shape[0]
    chips = points_ref.shape[0] // rows
    first = pl.multiple_of(lax.rem(at_ref[0] + shift, chips) * rows, rows)
    return pltpu.make_async_copy(points_ref.at[pl.ds(first, rows), :], next_ref, sem)


def prep_body(at_ref, l_ref, c_ref, points_ref, b_ref, cc_ref, next_ref, sem, *, shift):
    copy = fetched(at_ref, shift, points_ref, next_ref, sem)

    @pl.when(pl.program_id(0) == 0)
    def _():
        copy.start()

    rows, feats = l_ref.shape
    unit = math.log2(math.e) / feats
    mark = l_ref[...]
    high, low = halves(mark * (2.0 * unit))
    b_ref[:, :feats] = high
    b_ref[:, feats : 2 * feats] = low
    b_ref[:, 2 * feats : 3 * feats] = high
    norm = thirds(-unit * jnp.sum(mark * mark, axis=1, keepdims=True))
    b_ref[:, 3 * feats :] = norm_lanes(rows, [1.0, 1.0, 1.0, *norm])
    high, low = halves(c_ref[...])
    cc_ref[:, : high.shape[1]] = high
    cc_ref[:, high.shape[1] :] = low

    @pl.when(pl.program_id(0) == pl.num_programs(0) - 1)
    def _():
        copy.wait()


def prep(at, shift, landmarks, coefficients, points, held_rows, block=1024):
    marks, feats = landmarks.shape
    classes = coefficients.shape[1]
    wide = 3 * feats + LANES
    return pl.pallas_call(
        functools.partial(prep_body, shift=shift),
        grid_spec=pltpu.PrefetchScalarGridSpec(
            num_scalar_prefetch=1,
            grid=(marks // block,),
            in_specs=[
                pl.BlockSpec((block, feats), lambda i, s: (i, 0)),
                pl.BlockSpec((block, classes), lambda i, s: (i, 0)),
                pl.BlockSpec(memory_space=pl.ANY),
            ],
            out_specs=[
                pl.BlockSpec((block, wide), lambda i, s: (i, 0)),
                pl.BlockSpec((block, 2 * classes), lambda i, s: (i, 0)),
                pl.BlockSpec((held_rows, feats), lambda i, s: (0, 0)),
            ],
            scratch_shapes=[pltpu.SemaphoreType.DMA(())],
        ),
        out_shape=[
            pltpu.VMEM((marks, wide), bf16),
            pltpu.VMEM((marks, 2 * classes), bf16),
            pltpu.VMEM((held_rows, feats), f32),
        ],
        compiler_params=pltpu.CompilerParams(vmem_limit_bytes=12 << 20),
        name="prep",
    )(at, landmarks, coefficients, points)


def logits_body(at_ref, p_ref, b_ref, c_ref, *refs, tile, later):
    if later is None:
        hi_ref, lo_ref, far_ref, own_ref, a_ref = refs
    else:
        points_ref, hi_ref, lo_ref, far_ref, own_ref, next_ref, a_ref, sem = refs
        copy = fetched(at_ref, later, points_ref, next_ref, sem)

        @pl.when(pl.program_id(0) == 0)
        def _():
            copy.start()

    rows, feats = p_ref.shape
    marks = b_ref.shape[0]
    unit = math.log2(math.e) / feats
    point = p_ref[...]
    high, low = halves(point)
    a_ref[:, :feats] = high
    a_ref[:, feats : 2 * feats] = high
    a_ref[:, 2 * feats : 3 * feats] = low
    norm = thirds(-unit * jnp.sum(point * point, axis=1, keepdims=True))
    a_ref[:, 3 * feats :] = norm_lanes(rows, [*norm, 1.0, 1.0, 1.0])
    for j in range(marks // tile):
        cols = slice(j * tile, (j + 1) * tile)
        power = lax.dot_general(a_ref[...], b_ref[cols, :], NT, preferred_element_type=f32)
        kernel = jnp.exp2(power)
        high, low = halves(kernel)
        hi_ref[:, cols] = high
        lo_ref[:, cols] = low
    sums = []
    for u in range(2):
        part = slice(u * rows // 2, (u + 1) * rows // 2)
        both = dot(hi_ref[part, :], c_ref[...]) + dot(lo_ref[part, :], c_ref[...])
        sums.append(both[:, : both.shape[1] // 2] + both[:, both.shape[1] // 2 :])

    @pl.when(pl.program_id(0) == 0)
    def _():
        far_ref[...] = jnp.concatenate(sums, axis=0)

    @pl.when(pl.program_id(0) == 1)
    def _():
        own_ref[...] = jnp.concatenate(sums, axis=0)
        if later is not None:
            copy.wait()


def kernel_and_logits(at, held, wide_marks, wide_coefs, points, later, tile=512):
    rows, feats = held.shape
    block = rows // 2
    marks, wide = wide_marks.shape
    classes = wide_coefs.shape[1] // 2
    fixed = pl.Buffered(1)
    fetch = later is not None
    return pl.pallas_call(
        functools.partial(logits_body, tile=tile, later=later),
        grid_spec=pltpu.PrefetchScalarGridSpec(
            num_scalar_prefetch=1,
            grid=(2,),
            in_specs=[
                pl.BlockSpec((block, feats), lambda i, s: (lax.rem(s[1] + 1 + i, 2), 0)),
                pl.BlockSpec((marks, wide), lambda i, s: (0, 0), pipeline_mode=fixed),
                pl.BlockSpec((marks, 2 * classes), lambda i, s: (0, 0), pipeline_mode=fixed),
                *[pl.BlockSpec(memory_space=pl.ANY)] * fetch,
            ],
            out_specs=[
                pl.BlockSpec((block, marks), lambda i, s: (i, 0)),
                pl.BlockSpec((block, marks), lambda i, s: (i, 0)),
                pl.BlockSpec((block, classes), lambda i, s: (0, 0)),
                pl.BlockSpec((block, classes), lambda i, s: (0, 0)),
                *[pl.BlockSpec((rows, feats), lambda i, s: (0, 0))] * fetch,
            ],
            scratch_shapes=[
                pltpu.VMEM((block, wide), bf16),
                *[pltpu.SemaphoreType.DMA(())] * fetch,
            ],
        ),
        out_shape=[
            pltpu.VMEM((rows, marks), bf16),
            pltpu.VMEM((rows, marks), bf16),
            pltpu.VMEM((block, classes), f32),
            pltpu.VMEM((block, classes), f32),
            *[pltpu.VMEM((rows, feats), f32)] * fetch,
        ],
        compiler_params=pltpu.CompilerParams(vmem_limit_bytes=LIMIT_K1 << 20),
        cost_estimate=pl.CostEstimate(
            flops=2 * rows * marks * (wide + 4 * classes),
            bytes_accessed=4 * rows * (feats + marks + classes) + 2 * marks * (wide + 2 * classes),
            transcendentals=rows * marks,
        ),
        name="kernel_and_logits",
    )(at, held, wide_marks, wide_coefs, *[points] * fetch)


def block_and_logits(at, which, held, wide_marks, wide_coefs, tile=512):
    feats = held.shape[1]
    block = held.shape[0] // 2
    marks, wide = wide_marks.shape
    classes = wide_coefs.shape[1] // 2
    fixed = pl.Buffered(1)

    def body(at_ref, p_ref, b_ref, c_ref, hi_ref, lo_ref, out_ref, a_ref):
        logits_body(
            at_ref, p_ref, b_ref, c_ref, hi_ref, lo_ref, out_ref, out_ref, a_ref, tile=tile, later=None
        )

    return pl.pallas_call(
        body,
        grid_spec=pltpu.PrefetchScalarGridSpec(
            num_scalar_prefetch=1,
            grid=(1,),
            in_specs=[
                pl.BlockSpec((block, feats), lambda i, s: (lax.rem(s[1] + 1 + which, 2), 0)),
                pl.BlockSpec((marks, wide), lambda i, s: (0, 0), pipeline_mode=fixed),
                pl.BlockSpec((marks, 2 * classes), lambda i, s: (0, 0), pipeline_mode=fixed),
            ],
            out_specs=[
                pl.BlockSpec((block, marks), lambda i, s: (0, 0)),
                pl.BlockSpec((block, marks), lambda i, s: (0, 0)),
                pl.BlockSpec((block, classes), lambda i, s: (0, 0)),
            ],
            scratch_shapes=[pltpu.VMEM((block, wide), bf16)],
        ),
        out_shape=[
            pltpu.VMEM((block, marks), bf16),
            pltpu.VMEM((block, marks), bf16),
            pltpu.VMEM((block, classes), f32),
        ],
        compiler_params=pltpu.CompilerParams(vmem_limit_bytes=LIMIT_K1 << 20),
        cost_estimate=pl.CostEstimate(
            flops=2 * block * classes, bytes_accessed=4 * block * classes, transcendentals=0
        ),
        name="block_and_logits",
    )(at, held, wide_marks, wide_coefs)


def small_kernel(body, at, args, outs, name):
    whole = [pl.BlockSpec(x.shape, lambda i, s: (0, 0)) for x in (*args, *outs)]
    return pl.pallas_call(
        body,
        grid_spec=pltpu.PrefetchScalarGridSpec(
            num_scalar_prefetch=1,
            grid=(1,),
            in_specs=whole[: len(args)],
            out_specs=whole[len(args) :],
        ),
        out_shape=outs,
        compiler_params=pltpu.CompilerParams(vmem_limit_bytes=6 << 20),
        name=name,
    )(at, *args)


def ridge_body(at_ref, c_ref, out_ref):
    out_ref[...] = RIDGE * c_ref[...]


def own_ridge(at, coefficients):
    marks, classes = coefficients.shape
    kept = marks // lax.axis_size(PTS)
    return pl.pallas_call(
        ridge_body,
        grid_spec=pltpu.PrefetchScalarGridSpec(
            num_scalar_prefetch=1,
            grid=(1,),
            in_specs=[pl.BlockSpec((kept, classes), lambda i, s: (s[2], 0))],
            out_specs=pl.BlockSpec((kept, classes), lambda i, s: (0, 0)),
        ),
        out_shape=pltpu.VMEM((kept, classes), f32),
        compiler_params=pltpu.CompilerParams(vmem_limit_bytes=2 << 20),
        name="ridge",
    )(at, pltpu.with_memory_space_constraint(coefficients, pltpu.HBM))


def residual_body(at_ref, labels_ref, a_ref, b_ref, out_ref):
    logits = a_ref[...] + b_ref[...]
    rows, classes = logits.shape
    groups = rows // LANES
    expo = jnp.exp(logits)
    share = expo / jnp.sum(expo, axis=1, keepdims=True)
    base = (at_ref[0] * 2 + at_ref[1]) * groups
    for g in range(groups):
        label = jnp.broadcast_to(labels_ref[pl.ds(base + g, 1), :], (LANES, LANES)).T
        hot = label == lax.broadcasted_iota(jnp.int32, (LANES, classes), 1)
        part = slice(g * LANES, (g + 1) * LANES)
        out_ref[part, :] = share[part, :] - hot.astype(f32)


def terms_body(*refs, sets, pieces, tile):
    width = pieces + 2
    parts, (*before, out_ref, rt_ref) = refs[: width * sets], refs[width * sets :]
    block, classes = parts[0].shape
    marks = parts[pieces].shape[1]
    for n in range(sets):
        for h in range(pieces):
            resid = parts[width * n + h][...]
            high = resid.astype(bf16).astype(f32)
            rows = slice((pieces * n + h) * block, (pieces * n + h + 1) * block)
            rt_ref[:classes, rows] = high.T.astype(bf16)
            rt_ref[classes:, rows] = (resid - high).T.astype(bf16)
    for j in range(marks // tile):
        cols = slice(j * tile, (j + 1) * tile)
        both, small = None, None
        for n in range(sets):
            rows = slice(pieces * n * block, pieces * (n + 1) * block)
            term = dot(rt_ref[:, rows], parts[width * n + pieces][:, cols])
            both = term if both is None else both + term
            term = dot(rt_ref[:classes, rows], parts[width * n + pieces + 1][:, cols])
            small = term if small is None else small + term
        out = (both[:classes, :] + both[classes:, :] + small).T
        for ref in before:
            out = out + ref[cols, :]
        out_ref[cols, :] = out


def terms(sets, before=None, tile=1024):
    args = [x for one in sets for x in one]
    block, classes = args[0].shape
    pieces = len(sets[0]) - 2
    marks = args[pieces].shape[1]
    rows = pieces * block * len(sets)
    if before is not None:
        args.append(before)
    return pl.pallas_call(
        functools.partial(terms_body, sets=len(sets), pieces=pieces, tile=tile),
        in_specs=[pl.BlockSpec(memory_space=pltpu.VMEM)] * len(args),
        out_specs=pl.BlockSpec(memory_space=pltpu.VMEM),
        out_shape=pltpu.VMEM((marks, classes), f32),
        scratch_shapes=[pltpu.VMEM((2 * classes, rows), bf16)],
        compiler_params=pltpu.CompilerParams(vmem_limit_bytes=LIMIT_K2 << 20),
        cost_estimate=pl.CostEstimate(
            flops=8 * rows * marks * classes,
            bytes_accessed=4 * rows * (marks + classes) + 8 * marks * classes,
            transcendentals=0,
        ),
        name="terms",
    )(*args)


def swapped(x):
    return lax.ppermute(x, "core", [(0, 1), (1, 0)])


def summed_share(x, axes):
    devices = lax.axis_size(axes)
    parts = x.reshape(devices, x.shape[0] // devices, x.shape[1])
    return lax.all_to_all(parts, axes, split_axis=0, concat_axis=0, tiled=True).sum(axis=0)


def all_shares(x, axes):
    devices = lax.axis_size(axes)
    copies = jnp.broadcast_to(x, (devices, *x.shape))
    parts = lax.all_to_all(copies, axes, split_axis=0, concat_axis=0, tiled=True)
    return parts.reshape(devices * x.shape[0], x.shape[1])


def along_x(x, shift):
    chips = lax.axis_size("x")
    return lax.ppermute(x, "x", [(i, (i + shift) % chips) for i in range(chips)])


def across_z(x):
    return lax.ppermute(x, "zh", [(0, 1), (1, 0)])


def per_device(points, labels, landmarks, coefficients):
    chips = lax.axis_size("x")
    classes = coefficients.shape[1]
    block = points.shape[0] // (2 * chips)
    at = jnp.stack([lax.axis_index(n) for n in ("x", "core", PTS)]).astype(jnp.int32)
    points, landmarks, first_coefs = (
        pltpu.with_memory_space_constraint(x, pltpu.HBM) for x in (points, landmarks, coefficients)
    )
    at, landmarks = lax.optimization_barrier((at, landmarks))
    wide_marks, wide_coefs, held = prep(at, 2, landmarks, first_coefs, points, 2 * block)
    made, mine, arrived, sums = {}, {}, {}, []
    for shift, later, ready in ((2, 1, ()), (1, 3, (2,)), (3, 0, (1, 3))):
        hi, lo, far, own, *after = kernel_and_logits(at, held, wide_marks, wide_coefs, points, later)
        held = after[0]
        made[shift] = hi, lo
        mine[shift], arrived[shift] = own, swapped(far)
        both = [mine[n] + arrived[n] for n in ready]
        if both:
            at, both = lax.optimization_barrier((at, both))
        sums += [along_x(x, n) for x, n in zip(both, ready)]
    *far_made, far = block_and_logits(at, 0, held, wide_marks, wide_coefs)
    over = swapped(far)
    at, far = lax.optimization_barrier((at, far))
    *own_made, own = block_and_logits(at, 1, held, wide_marks, wide_coefs)
    logits = own + over + sums[0] + sums[1] + sums[2]
    full = jax.ShapeDtypeStruct((block, classes), f32)
    by_group = labels.reshape(-1, LANES)
    (own,) = small_kernel(residual_body, at, [by_group, logits, across_z(logits)], [full], "residual")
    near = {3: along_x(own, 1), 1: along_x(own, 3)}
    local = terms([(swapped(own), *far_made), (own, *own_made)])
    at, local = lax.optimization_barrier((at, local))
    ridge = own_ridge(at, coefficients)
    local, near, ridge = lax.optimization_barrier((local, near, ridge))
    front, back = along_x(near[3][: block // 2], 1), along_x(near[1][block // 2 :], 3)
    local = terms([(swapped(near[n]), near[n], *made[n]) for n in (3, 1)], local)
    local, front, back = lax.optimization_barrier((local, front, back))
    last = jnp.concatenate([front, back], axis=0)
    local = terms([(swapped(last), last, *made[2])], local)
    total_points = labels.shape[0] * lax.axis_size(PTS)
    share = summed_share(local, PTS)
    return all_shares(share * (LOSS_SCALE / total_points) + ridge, PTS)


def solution(mesh):
    fine = Mesh(mesh.devices.reshape(4, 2, 2, 4, 2), AXES)
    in_specs = (P(PTS, None), P(PTS), P(LMK, None), P(LMK, None))
    return jax.shard_map(
        per_device, mesh=fine, in_specs=in_specs, out_specs=P(LMK, None), check_vma=False
    )
```
